256 devices in a mesh: dp: 16 (over x_lo, z), tensor: 16 (over x_hi, y, core).
Axes of the slice: x: 4 (x_hi: 2, x_lo: 2; x = x_hi * 2 + x_lo), y: 4, z: 8, core: 2. Of those that a mesh axis runs over, the one named last changes fastest.
Arguments:
- hidden: bfloat16 [4096, 8192], P('dp', 'tensor'), may hold values from -6 to 6
- connector: bfloat16 [8192, 3584], P('tensor'), may hold values from -0.0625 to 0.0625
- routing: int32 [4096, 1], P('dp'), may hold values from 0 to 15; in each aligned block of 256 rows (0 to 255, 256 to 511, ...) at most 32 rows name the same one
- talker_in: bfloat16 [8192, 3584], P(('dp', 'tensor')), may hold values from -6 to 6
- norm_gain: float32 [3584], replicated, may hold values from 0.25 to 1.75
- kv_weight: bfloat16 [3584, 1024], replicated, may hold values from -0.09375 to 0.09375
- kv_grad: bfloat16 [8192, 1024], P(('dp', 'tensor')), may hold values from -24 to 24
Outputs:
- hidden_grad: bfloat16 [4096, 8192], P('dp', 'tensor')
- connector_grad: float32 [8192, 3584], P('tensor', 'dp')
- kv_weight_grad: float32 [3584, 1024], P(None, ('dp', 'tensor'))
The draws below stay inside these ranges and needn't reach their ends.
Inputs may be any that keep to these rules, and one draw needn't show every extreme that they name: `routing`: among the 256 rows of one index of dp, at most 32 go to one shard.
All inputs are finite; a program needn't handle non-finite values.
Results may differ from the reference program's by a relative error of at most 0.005.
Values may be sent and summed in bfloat16 or wider, within the bound.
A program may use at most 64 MiB of HBM per device.

```python
import math
import jax
import jax.numpy as jnp
import numpy as np
from jax import lax

D = 8192
DT = 3584
KVW = 1024
TOK_DEV = 256
CAP = 32
TOKENS = 4096
SLOTS = 8192
N_DP = 16
N_TENSOR = 16


def raised(result, key, source, target, parts, factor):
    owner, partner = [(jnp.arange(result.shape[position]) // (result.shape[position] // parts)).reshape([-1 if axis == position else 1 for axis in range(result.ndim)]) for position in (source, target)]
    chosen = jax.random.permutation(key, parts)[partner]
    strong = (owner == chosen) | (owner == (partner + parts // 2) % parts)
    return jnp.where(strong, factor * result, result)


def shard_levels(stream_key, dims, split, low, high):
    level = 1.0
    for dim, blocks in split:
        heights = jax.random.uniform(jax.random.fold_in(jax.random.fold_in(stream_key, 6), dim), (blocks,), jnp.float32, low / len(split), high / len(split))
        level = level * jnp.repeat(jnp.exp(heights), dims[dim] // blocks).reshape((-1,) + (1,) * (len(dims) - 1 - dim))
    return level


def assign_block(key, own, number, rows, count, top, most, slope):
    order = jax.random.permutation(key, count)
    heavy_load, ordinary = shares(count, rows * top, most, slope, True), shares(count, rows * top, most, slope, False)
    places = jnp.arange(count)

    def named(lengths, turn):
        used = int((lengths > 0).sum())
        fixed = max(1, used // 4)
        shifted = fixed + (places - fixed + turn * (used - fixed)) % max(1, count - fixed)
        return jnp.zeros((count,), jnp.int32).at[order[jnp.where(places < fixed, places, shifted)]].set(jnp.asarray(lengths, jnp.int32))

    lengths = jnp.where(number % 4 == 0, named(heavy_load, number // 4), named(ordinary, number - number // 4 - 1))
    mixed = jax.random.permutation(jax.random.fold_in(own, 3), count)
    giver, receiver = mixed[0:count // 2 * 2:2], mixed[1:count // 2 * 2:2]
    slack = jnp.minimum(lengths[giver] - 1, most - lengths[receiver]) // 2
    slack = jnp.where((giver == order[0]) | (receiver == order[0]) | (lengths[receiver] == 0), 0, jnp.maximum(slack, 0))
    shifted = jax.random.randint(jax.random.fold_in(own, 4), (count // 2,), 0, 1 << 20) % (slack + 1)
    lengths = lengths.at[giver].add(-shifted).at[receiver].add(shifted)
    items = jnp.searchsorted(jnp.cumsum(lengths), jnp.arange(rows * top), side="right").astype(jnp.int32)
    listing = items.reshape(top, rows).T
    listing = listing[jax.random.permutation(jax.random.fold_in(own, 1), rows)]
    turn = jax.random.randint(jax.random.fold_in(own, 2), (rows, 1), 0, top)
    return jnp.take_along_axis(listing, (jnp.arange(top)[None, :] + turn) % top, axis=1)


def shares(amount, total, reach, lean, full):
    loads = [(1 << 20) // math.isqrt(standing ** lean) + 1 for standing in range(1, amount + 1)]
    largest = reach if full else min(reach, max(-(-total // amount), total * loads[0] // sum(loads)))
    least = 1 if total - largest >= amount - 1 else 0
    holding, rest = [largest] + [least] * (amount - 1), total - largest - least * (amount - 1)
    while rest > 0:
        free = [i for i in range(1, amount) if holding[i] < largest] or [i for i in range(1, amount) if holding[i] < reach]
        whole, budget = sum([loads[i] for i in free]), rest
        for i in free:
            extra = min(reach - holding[i], max(1, budget * loads[i] // whole), rest)
            holding[i] = holding[i] + extra
            rest = rest - extra
    return np.array(holding)


def bell_draw(stream_key, shape, scale, limit, split=(), kind=jnp.bfloat16):
    values = scale * jax.random.normal(stream_key, shape, jnp.float32)
    if split:
        values = values * shard_levels(stream_key, shape, split, -0.22, 0.18)
    return jnp.clip(values, -limit, limit).astype(kind)


def bell_draw_with(stream_key, extent, spread, most, cuts, heavy, kind=jnp.bfloat16):
    result = spread * jax.random.normal(stream_key, extent, jnp.float32)
    if cuts:
        result = result * shard_levels(stream_key, extent, cuts, -0.22, 0.18)
    return jnp.clip(raised(result, jax.random.fold_in(stream_key, 3), *heavy), -most, most).astype(kind)


def setup_inputs(seed: int = 0) -> dict:
    keys = jax.random.split(jax.random.key(seed), 8)
    hidden = bell_draw(keys[0], (TOKENS, D), 1.0, 6.0, ((0, 16), (1, 16)))
    connector = bell_draw(keys[1], (D, DT), D ** -0.5, 0.0625, ((0, 16),))
    routing_keys = jax.random.split(jax.random.fold_in(keys[2], 1), TOKENS // TOK_DEV)
    routing_turns = jax.random.permutation(jax.random.fold_in(keys[2], 3), TOKENS // TOK_DEV)
    routing = jax.vmap(lambda own, number: assign_block(jax.random.fold_in(keys[2], 2), own, number, TOK_DEV, N_TENSOR, 1, CAP, 1))(routing_keys, routing_turns).reshape((TOKENS, 1))
    talker_in = bell_draw(keys[3], (SLOTS, DT), 1.0, 6.0, ((0, 256),))
    norm_gain = jnp.clip(1.0 + 0.15 * jax.random.normal(keys[4], (DT,), jnp.float32), 0.25, 1.75)
    kv_weight = bell_draw(keys[5], (DT, KVW), DT ** -0.5, 0.09375)
    kv_grad = bell_draw_with(keys[6], (SLOTS, KVW), 1.0, 24.0, ((0, 256),), (0, 1, 256, 6.0))
    return {"hidden": hidden, "connector": connector, "routing": routing, "talker_in": talker_in, "norm_gain": norm_gain, "kv_weight": kv_weight, "kv_grad": kv_grad}


def slot_index(group_routes):
    shards = jnp.arange(N_TENSOR, dtype=jnp.int32)
    onehot = (group_routes[:, None] == shards[None, :]).astype(jnp.int32)
    ranks = lax.optimization_barrier(jnp.sum((jnp.cumsum(onehot, axis=0) - 1) * onehot, axis=1))
    return ((group_routes * CAP + ranks).astype(jnp.int32), lax.optimization_barrier(jnp.sum(onehot, axis=0)).astype(jnp.int32))

def pick_rows(table, indices):
    return jnp.take(table, indices, axis=0)

def reference(hidden, connector, routing, talker_in, norm_gain, kv_weight, kv_grad):
    group_routes = routing[:, 0].reshape(N_DP, TOK_DEV)
    slot_ids, counts = jax.vmap(slot_index)(group_routes)
    usable = (jnp.arange(CAP, dtype=jnp.int32)[None, None, :] < counts[:, :, None]).reshape(SLOTS)
    masked = jnp.where(usable[:, None], kv_grad, jnp.zeros_like(kv_grad))
    inputs = talker_in.astype(jnp.float32)
    inv_rms = lax.rsqrt(lax.optimization_barrier(jnp.mean(inputs * inputs, axis=1, keepdims=True)) + 1e-06)
    scaled = inputs * inv_rms
    normed = (scaled * norm_gain).astype(jnp.bfloat16)
    factor = 1.0 / math.sqrt(TOKENS)
    kv_weight_grad = jnp.dot(normed.T, masked, preferred_element_type=jnp.float32) * factor
    back_grad = jnp.dot(masked, kv_weight.T, preferred_element_type=jnp.float32)
    gain_back = norm_gain * back_grad
    talker_grad = (inv_rms * (gain_back - scaled * lax.optimization_barrier(jnp.mean(gain_back * scaled, axis=1, keepdims=True)))).astype(jnp.bfloat16)
    grouped = talker_grad.reshape(N_DP, N_TENSOR * CAP, DT)
    row_grad = jax.vmap(pick_rows)(grouped, slot_ids).reshape(TOKENS, DT)
    hidden_grad = jnp.dot(row_grad, connector.T, preferred_element_type=jnp.float32).astype(jnp.bfloat16)
    connector_grad = jnp.dot(hidden.T, row_grad, preferred_element_type=jnp.float32) * factor
    return (hidden_grad, connector_grad, kv_weight_grad)
```

```python
import math

import jax
import jax.numpy as jnp
from jax import lax
from jax.experimental import pallas as pl
from jax.experimental.pallas import tpu as pltpu
from jax.sharding import PartitionSpec as P

MESH = pl.DeviceIdType.MESH
CONTRACT_LAST = (((1,), (1,)), ((), ()))
CONTRACT_FIRST = (((0,), (0,)), ((), ()))

NZ = 8
NY = 4


class Place:
    def __init__(self):
        self.dp = lax.axis_index("dp")
        self.t = lax.axis_index("tensor")
        self.z = lax.rem(self.dp, NZ)
        self.xl = lax.div(self.dp, NZ)
        self.core = lax.rem(self.t, 2)
        self.y = lax.rem(lax.div(self.t, 2), NY)
        self.xh = lax.div(self.t, 2 * NY)

    def tensor(self, xh, y, core):
        return xh * (2 * NY) + lax.rem(y + NY, NY) * 2 + core

    def at_y(self, step):
        return (self.dp, self.tensor(self.xh, self.y + step, self.core))

    def at_z(self, step):
        return (self.xl * NZ + lax.rem(self.z + step + NZ, NZ), self.t)

    def across(self):
        return (self.dp, self.tensor(1 - self.xh, self.y, self.core))

    def sibling(self):
        return (self.dp, self.tensor(self.xh, self.y, 1 - self.core))


def greet(devices):
    barrier = pltpu.get_barrier_semaphore()
    for device in devices:
        pl.semaphore_signal(barrier, inc=1, device_id=device, device_id_type=MESH)
    pl.semaphore_wait(barrier, len(devices))


class Sends:
    def __init__(self, send_sems, recv_sems):
        self.send_sems, self.recv_sems = send_sems, recv_sems
        self.open = []

    def send(self, src, dst, key, device):
        copy = pltpu.make_async_remote_copy(
            src_ref=src,
            dst_ref=dst,
            send_sem=self.send_sems.at[key],
            recv_sem=self.recv_sems.at[key],
            device_id=device,
            device_id_type=MESH,
        )
        copy.start()
        self.open.append(copy)

    def arrived(self, dst, key, device):
        pltpu.make_async_remote_copy(
            src_ref=dst,
            dst_ref=dst,
            send_sem=self.send_sems.at[key],
            recv_sem=self.recv_sems.at[key],
            device_id=device,
            device_id_type=MESH,
        ).wait_recv()

    def drain(self):
        for copy in self.open:
            copy.wait_send()


GROUP_KEYS = 12 + 2 + 16


def key_y(direction, far, kind):
    return direction * 6 + far * 3 + kind


def key_x(half):
    return 12 + half


def key_s(hop, half):
    return 14 + hop * 2 + half


class GroupGather:
    def __init__(self, place, own, slot, sends, base):
        self.place, self.own, self.slot = place, own, slot
        self.sends, self.base = sends, base

    def block(self, far, step):
        p = self.place
        return p.tensor(1 - p.xh if far else p.xh, p.y + step, p.core)

    def twin(self, far, step):
        p = self.place
        return p.tensor(1 - p.xh if far else p.xh, p.y + step, 1 - p.core)

    def hop(self, far, step):
        return far * 4 + step % 4

    def share(self, src, far, step, half):
        self.sends.send(
            src,
            self.slot(self.block(far, step), half),
            self.base + key_s(self.hop(far, step), half),
            self.place.sibling(),
        )

    def to_y(self, src, far, half, direction):
        step = 1 if direction == 0 else -1
        self.sends.send(
            src,
            self.slot(self.block(far, 0), half),
            self.base + key_y(direction, far, half),
            self.place.at_y(step),
        )

    def start(self):
        for half in (0, 1):
            self.to_y(self.own(half), 0, half, 0)
            self.to_y(self.own(1 - half), 0, 1 - half, 1)
            self.sends.send(
                self.own(half),
                self.slot(self.block(0, 0), half),
                self.base + key_x(half),
                self.place.across(),
            )
        for half in (0, 1):
            self.share(self.own(half), 0, 0, half)

    def take_x(self, half):
        dst = self.slot(self.block(1, 0), half)
        self.sends.arrived(dst, self.base + key_x(half), self.place.across())
        self.to_y(dst, 1, half, 0)
        self.to_y(dst, 1, half, 1)
        self.share(dst, 1, 0, half)

    def take_y(self, far, half, direction):
        step = -1 if direction == 0 else 1
        dst = self.slot(self.block(far, step), half)
        self.sends.arrived(
            dst, self.base + key_y(direction, far, half), self.place.at_y(step)
        )
        if half == direction:
            self.sends.send(
                dst,
                dst,
                self.base + key_y(direction, far, 2),
                self.place.at_y(-step),
            )
        self.share(dst, far, step, half)

    def take_far(self, far, direction):
        step = -1 if direction == 0 else 1
        half = direction
        dst = self.slot(self.block(far, 2 * step), half)
        self.sends.arrived(
            dst, self.base + key_y(direction, far, 2), self.place.at_y(step)
        )
        self.share(dst, far, 2, half)

    def take_shared(self):
        for far in (0, 1):
            for step in (0, 1, 2, 3):
                for half in (0, 1):
                    self.sends.arrived(
                        self.slot(self.twin(far, step), half),
                        self.base + key_s(self.hop(far, step), half),
                        self.place.sibling(),
                    )


def gather_inputs(talker_ref, kv_ref, hidden_ref, talkers, kvs, hiddens, send_sems, recv_sems, own_sems):
    place = Place()
    greet(
        [place.at_y(1), place.at_y(-1), place.across(), place.sibling(), place.at_z(1), place.at_z(-1)]
    )
    sends = Sends(send_sems, recv_sems)
    half_rows = talker_ref.shape[0] // 2
    half_hidden = hidden_ref.shape[0] // 2
    kept = [
        pltpu.make_async_copy(talker_ref, talkers.at[place.t], own_sems.at[0]),
        pltpu.make_async_copy(kv_ref, kvs.at[place.t], own_sems.at[1]),
        pltpu.make_async_copy(hidden_ref, hiddens.at[place.z], own_sems.at[2]),
    ]

    def gather(own_ref, slots, base):
        return GroupGather(
            place,
            lambda half: own_ref.at[pl.ds(half * half_rows, half_rows)],
            lambda block, half: slots.at[block, pl.ds(half * half_rows, half_rows)],
            sends,
            base,
        )

    pair = (gather(talker_ref, talkers, 0), gather(kv_ref, kvs, GROUP_KEYS))
    z_base = 2 * GROUP_KEYS

    def z_slot(step, part=None):
        slot = hiddens.at[lax.rem(place.z + step + NZ, NZ)]
        if part is None:
            return slot
        return slot.at[pl.ds(part * half_hidden, half_hidden)]

    def pass_z(hop):
        for direction, step in ((0, -1), (1, 1)):
            if hop:
                sends.arrived(z_slot(hop * step), z_base + direction * 4 + hop - 1, place.at_z(step))
            part = direction if hop == 3 else None
            if hop:
                src = z_slot(hop * step, part)
            else:
                src = hidden_ref
            sends.send(
                src, z_slot(hop * step, part), z_base + direction * 4 + hop, place.at_z(-step)
            )

    pass_z(0)
    for g in pair:
        g.start()
    for copy in kept:
        copy.start()
    for direction in (0, 1):
        for g in pair:
            g.take_y(0, direction, direction)
    for g in pair:
        g.take_x(0)
    pass_z(1)
    for direction in (0, 1):
        for g in pair:
            g.take_y(0, 1 - direction, direction)
    for g in pair:
        g.take_x(1)
    for direction in (0, 1):
        for g in pair:
            g.take_far(0, direction)
    pass_z(2)
    for half in (0, 1):
        for direction in (0, 1):
            for g in pair:
                g.take_y(1, half, direction)
    pass_z(3)
    for direction in (0, 1):
        for g in pair:
            g.take_far(1, direction)
    for g in pair:
        g.take_shared()
    for direction, step in ((0, -1), (1, 1)):
        sends.arrived(z_slot(4 * step, direction), z_base + direction * 4 + 3, place.at_z(step))
    for copy in kept:
        copy.wait()
    sends.drain()


def exchange_terms(rows_ref, terms_ref, gathered, received, send_sems, recv_sems, own_sems):
    place = Place()
    n_dp = terms_ref.shape[0]

    def peer(step):
        return lax.rem(place.dp + step, n_dp)

    others = [(peer(step), place.t) for step in range(1, n_dp)]
    greet(others + [place.at_y(1), place.at_y(-1), place.across(), place.sibling()])
    sends = Sends(send_sems, recv_sems)
    kept = [
        pltpu.make_async_copy(
            rows_ref.at[place.z], gathered.at[:, place.z, place.t], own_sems.at[0]
        ),
        pltpu.make_async_copy(
            terms_ref.at[place.dp], received.at[place.dp], own_sems.at[1]
        ),
    ]
    for copy in kept:
        copy.start()
    z_base = GROUP_KEYS

    def z_from(step):
        return lax.rem(place.z + step + NZ, NZ)

    for step in (1, 7, 2, 6, 3, 5, 4):
        sends.send(
            rows_ref.at[z_from(step)],
            gathered.at[:, place.z, place.t],
            z_base + step,
            place.at_z(step),
        )
    kv_base = z_base + NZ
    for step in range(1, n_dp):
        sends.send(
            terms_ref.at[peer(step)],
            received.at[place.dp],
            kv_base + step,
            (peer(step), place.t),
        )
    for step in range(1, NZ):
        sends.arrived(
            gathered.at[:, z_from(-step), place.t], z_base + step, place.at_z(-step)
        )
    kept[0].wait()

    def slot(block, half):
        return gathered.at[half, :, block]

    g = GroupGather(place, lambda half: slot(place.t, half), slot, sends, 0)
    g.start()
    for direction in (0, 1):
        g.take_y(0, direction, direction)
    g.take_x(0)
    for direction in (0, 1):
        g.take_y(0, 1 - direction, direction)
    g.take_x(1)
    for direction in (0, 1):
        g.take_far(0, direction)
    for half in (0, 1):
        for direction in (0, 1):
            g.take_y(1, half, direction)
    for direction in (0, 1):
        g.take_far(1, direction)
    g.take_shared()
    for step in range(1, n_dp):
        sends.arrived(
            received.at[peer(n_dp - step)], kv_base + step, (peer(n_dp - step), place.t)
        )
    kept[1].wait()
    sends.drain()


VMEM = pl.BlockSpec(memory_space=pltpu.VMEM)
ANY = pl.BlockSpec(memory_space=pl.ANY)


def on_device(hidden, connector, routing, talker_in, norm_gain, kv_weight, kv_grad):
    n_dp = lax.axis_size("dp")
    n_tensor = lax.axis_size("tensor")
    rows_dev, d_dev = hidden.shape
    capacity, width = talker_in.shape
    kv_width = kv_grad.shape[1]
    factor = 1.0 / math.sqrt(rows_dev * n_dp)
    slots = n_tensor * capacity
    bf16 = jnp.bfloat16

    first = 2 * GROUP_KEYS + 8
    talkers, kvs, hiddens = pl.pallas_call(
        gather_inputs,
        out_shape=(
            jax.ShapeDtypeStruct((n_tensor, capacity, width), bf16),
            jax.ShapeDtypeStruct((n_tensor, capacity, kv_width), bf16),
            jax.ShapeDtypeStruct((NZ, rows_dev, d_dev), bf16),
        ),
        in_specs=[VMEM] * 3,
        out_specs=[ANY] * 3,
        scratch_shapes=[
            pltpu.SemaphoreType.DMA((first,)),
            pltpu.SemaphoreType.DMA((first,)),
            pltpu.SemaphoreType.DMA((3,)),
        ],
        compiler_params=pltpu.CompilerParams(collective_id=0, has_side_effects=True),
    )(talker_in, kv_grad, hidden)

    route = routing[:, 0]
    shards = jnp.arange(n_tensor, dtype=jnp.int32)
    named = (route[:, None] == shards[None, :]).astype(jnp.float32)
    earlier = jnp.arange(rows_dev)[:, None] > jnp.arange(rows_dev)[None, :]
    before = jnp.dot(earlier.astype(jnp.float32), named, preferred_element_type=jnp.float32)
    ranks = jnp.sum(before * named, axis=1).astype(jnp.int32)
    slot_ids = route * capacity + ranks
    pick = (slot_ids[:, None] == jnp.arange(slots, dtype=jnp.int32)[None, :]).astype(bf16)

    talker_rows = jnp.dot(pick, talkers.reshape(slots, width), preferred_element_type=jnp.float32)
    kv_rows = jnp.dot(
        pick, kvs.reshape(slots, kv_width), preferred_element_type=jnp.float32
    ).astype(bf16)
    inv_rms = lax.rsqrt(jnp.mean(talker_rows * talker_rows, axis=1, keepdims=True) + 1e-06)
    scaled = talker_rows * inv_rms
    normed = (scaled * norm_gain).astype(bf16)
    back_grad = lax.dot_general(
        kv_rows, kv_weight, CONTRACT_LAST, preferred_element_type=jnp.float32
    )
    gain_back = norm_gain * back_grad
    row_grad = (
        inv_rms * (gain_back - scaled * jnp.mean(gain_back * scaled, axis=1, keepdims=True))
    ).astype(bf16)

    t = lax.axis_index("tensor")
    slice_rows = rows_dev // n_tensor
    own_rows = lax.dynamic_slice_in_dim(row_grad, t * slice_rows, slice_rows, 0)
    own_rows = own_rows.reshape(slice_rows, n_dp // NZ, NZ, width // n_dp).transpose(2, 1, 0, 3)
    per_dev = kv_width // (n_dp * n_tensor)
    own_cols = lax.dynamic_index_in_dim(
        kv_rows.reshape(rows_dev, n_dp, n_tensor, per_dev), t, 2, keepdims=False
    ).reshape(rows_dev, n_dp * per_dev)
    terms = lax.dot_general(own_cols, normed, CONTRACT_FIRST, preferred_element_type=jnp.float32)
    terms = (terms * factor).astype(bf16).reshape(n_dp, per_dev, width)

    second = GROUP_KEYS + NZ + n_dp
    gathered, received = pl.pallas_call(
        exchange_terms,
        out_shape=(
            jax.ShapeDtypeStruct((n_dp // NZ, NZ, n_tensor, slice_rows, width // n_dp), bf16),
            jax.ShapeDtypeStruct((n_dp, per_dev, width), bf16),
        ),
        in_specs=[VMEM] * 2,
        out_specs=[ANY] * 2,
        scratch_shapes=[
            pltpu.SemaphoreType.DMA((second,)),
            pltpu.SemaphoreType.DMA((second,)),
            pltpu.SemaphoreType.DMA((2,)),
        ],
        compiler_params=pltpu.CompilerParams(collective_id=1, has_side_effects=True),
    )(own_rows, terms)

    hidden_grad = lax.dot_general(
        row_grad, connector, CONTRACT_LAST, preferred_element_type=jnp.float32
    ).astype(bf16)
    kv_weight_grad = jnp.sum(received.astype(jnp.float32), axis=0).T
    all_hidden = hiddens.reshape(NZ * rows_dev, d_dev)
    blocks = gathered.reshape(n_dp // NZ, NZ * rows_dev, width // n_dp)
    x_lo = lax.axis_index("dp") // NZ

    def part(block):
        rows = lax.dynamic_index_in_dim(blocks, block, 0, keepdims=False)
        return (
            lax.dot_general(all_hidden, rows, CONTRACT_FIRST, preferred_element_type=jnp.float32)
            * factor
        )

    away = part(1 - x_lo).astype(bf16)
    swapped = lax.ppermute(away, "dp", [(i, (i + NZ) % (2 * NZ)) for i in range(2 * NZ)])
    connector_grad = part(x_lo) + swapped.astype(jnp.float32)
    return (hidden_grad, connector_grad, kv_weight_grad)


def solution(mesh):
    return jax.shard_map(
        on_device,
        mesh=mesh,
        in_specs=(
            P("dp", "tensor"),
            P("tensor", None),
            P("dp", None),
            P(("dp", "tensor"), None),
            P(),
            P(),
            P(("dp", "tensor"), None),
        ),
        out_specs=(P("dp", "tensor"), P("tensor", "dp"), P(None, ("dp", "tensor"))),
        check_vma=False,
    )
```

```python
import math

import jax
import jax.numpy as jnp
from jax import lax
from jax.experimental import pallas as pl
from jax.experimental.pallas import tpu as pltpu
from jax.sharding import PartitionSpec as P

MESH = pl.DeviceIdType.MESH
CONTRACT_LAST = (((1,), (1,)), ((), ()))
CONTRACT_FIRST = (((0,), (0,)), ((), ()))

NZ = 8
NY = 4


class Place:
    def __init__(self):
        self.dp = lax.axis_index("dp")
        self.t = lax.axis_index("tensor")
        self.z = lax.rem(self.dp, NZ)
        self.xl = lax.div(self.dp, NZ)
        self.core = lax.rem(self.t, 2)
        self.y = lax.rem(lax.div(self.t, 2), NY)
        self.xh = lax.div(self.t, 2 * NY)

    def tensor(self, xh, y, core):
        return xh * (2 * NY) + lax.rem(y + NY, NY) * 2 + core

    def at_y(self, step):
        return (self.dp, self.tensor(self.xh, self.y + step, self.core))

    def at_z(self, step):
        return (self.xl * NZ + lax.rem(self.z + step + NZ, NZ), self.t)

    def across(self):
        return (self.dp, self.tensor(1 - self.xh, self.y, self.core))

    def sibling(self):
        return (self.dp, self.tensor(self.xh, self.y, 1 - self.core))


def greet(devices):
    barrier = pltpu.get_barrier_semaphore()
    for device in devices:
        pl.semaphore_signal(barrier, inc=1, device_id=device, device_id_type=MESH)
    pl.semaphore_wait(barrier, len(devices))


class Sends:
    def __init__(self, send_sems, recv_sems):
        self.send_sems, self.recv_sems = send_sems, recv_sems
        self.open = []

    def send(self, src, dst, key, device):
        copy = pltpu.make_async_remote_copy(
            src_ref=src,
            dst_ref=dst,
            send_sem=self.send_sems.at[key],
            recv_sem=self.recv_sems.at[key],
            device_id=device,
            device_id_type=MESH,
        )
        copy.start()
        self.open.append(copy)

    def arrived(self, dst, key, device):
        pltpu.make_async_remote_copy(
            src_ref=dst,
            dst_ref=dst,
            send_sem=self.send_sems.at[key],
            recv_sem=self.recv_sems.at[key],
            device_id=device,
            device_id_type=MESH,
        ).wait_recv()

    def drain(self):
        for copy in self.open:
            copy.wait_send()


GROUP_KEYS = 12 + 2 + 16


def key_y(direction, far, kind):
    return direction * 6 + far * 3 + kind


def key_x(half):
    return 12 + half


def key_s(hop, half):
    return 14 + hop * 2 + half


class GroupGather:
    def __init__(self, place, own, slot, sends, base):
        self.place, self.own, self.slot = place, own, slot
        self.sends, self.base = sends, base

    def block(self, far, step):
        p = self.place
        return p.tensor(1 - p.xh if far else p.xh, p.y + step, p.core)

    def twin(self, far, step):
        p = self.place
        return p.tensor(1 - p.xh if far else p.xh, p.y + step, 1 - p.core)

    def hop(self, far, step):
        return far * 4 + step % 4

    def share(self, src, far, step, half):
        self.sends.send(
            src,
            self.slot(self.block(far, step), half),
            self.base + key_s(self.hop(far, step), half),
            self.place.sibling(),
        )

    def to_y(self, src, far, half, direction):
        step = 1 if direction == 0 else -1
        self.sends.send(
            src,
            self.slot(self.block(far, 0), half),
            self.base + key_y(direction, far, half),
            self.place.at_y(step),
        )

    def start(self):
        for half in (0, 1):
            self.to_y(self.own(half), 0, half, 0)
            self.to_y(self.own(1 - half), 0, 1 - half, 1)
            self.sends.send(
                self.own(half),
                self.slot(self.block(0, 0), half),
                self.base + key_x(half),
                self.place.across(),
            )
        for half in (0, 1):
            self.share(self.own(half), 0, 0, half)

    def take_x(self, half):
        dst = self.slot(self.block(1, 0), half)
        self.sends.arrived(dst, self.base + key_x(half), self.place.across())
        self.to_y(dst, 1, half, 0)
        self.to_y(dst, 1, half, 1)
        self.share(dst, 1, 0, half)

    def take_y(self, far, half, direction):
        step = -1 if direction == 0 else 1
        dst = self.slot(self.block(far, step), half)
        self.sends.arrived(
            dst, self.base + key_y(direction, far, half), self.place.at_y(step)
        )
        if half == direction:
            self.sends.send(
                dst,
                dst,
                self.base + key_y(direction, far, 2),
                self.place.at_y(-step),
            )
        self.share(dst, far, step, half)

    def take_far(self, far, direction):
        step = -1 if direction == 0 else 1
        half = direction
        dst = self.slot(self.block(far, 2 * step), half)
        self.sends.arrived(
            dst, self.base + key_y(direction, far, 2), self.place.at_y(step)
        )
        self.share(dst, far, 2, half)

    def take_shared(self):
        for far in (0, 1):
            for step in (0, 1, 2, 3):
                for half in (0, 1):
                    self.sends.arrived(
                        self.slot(self.twin(far, step), half),
                        self.base + key_s(self.hop(far, step), half),
                        self.place.sibling(),
                    )


class GatherFromY(GroupGather):
    def start(self):
        for half in (0, 1):
            self.to_y(self.own(half), 0, half, 0)
            self.to_y(self.own(1 - half), 0, 1 - half, 1)
            self.to_x(self.own(half), 0, half)
        for half in (0, 1):
            self.share(self.own(half), 0, 0, half)

    def to_x(self, src, step, half):
        self.sends.send(
            src,
            self.slot(self.block(0, step), half),
            self.base + key_from_y(step, half),
            self.place.across(),
        )

    def take_y(self, far, half, direction):
        super().take_y(0, half, direction)
        step = -1 if direction == 0 else 1
        self.to_x(self.slot(self.block(0, step), half), step, half)

    def take_far(self, far, direction):
        super().take_far(0, direction)
        self.to_x(self.slot(self.block(0, 2), direction), 2, direction)

    def take_x(self, step, half):
        dst = self.slot(self.block(1, step), half)
        self.sends.arrived(dst, self.base + key_from_y(step, half), self.place.across())
        self.share(dst, 1, step, half)


def key_from_y(step, half):
    return (3, 4, 5, 9, 10, 11, 12, 13)[(step % 4) * 2 + half]


TILE = 512
BLOCK = 256
WINDOW = 384


def onehot(rows):
    return jnp.where(rows, 1.0, 0.0).astype(jnp.bfloat16)


def dot(a, b, contract):
    return lax.dot_general(a, b, (contract, ((), ())), preferred_element_type=jnp.float32)


NN = ((1,), (0,))
NT = ((1,), (1,))
TN = ((0,), (0,))


def whole(
    talker_ref, kv_ref, hidden_ref, gain_ref, ids_row_ref, ids_col_ref, weight_any, connector_any,
    hidden_grad_ref, connector_grad_ref, weight_grad_ref,
    talkers, kvs, hiddens, ids, weight, connector,
    local_back, local_grad, packed, blocks, ordered, pick, rows, kv_rows, back, columns, terms, terms_in,
    away, away_in, sums, sums_in, total, send_sems, recv_sems, own_sems,
):
    bf16, f32 = jnp.bfloat16, jnp.float32
    place = Place()
    width = talker_ref.shape[1]
    tiles = width // TILE
    capacity = talker_ref.shape[0]
    n_tensor = talkers.shape[0]
    slots = n_tensor * capacity
    rows_dev = hidden_ref.shape[0]
    factor = 1.0 / math.sqrt(rows_dev * 2 * NZ)
    loads = [
        pltpu.make_async_copy(weight_any, weight, own_sems.at[0]),
        pltpu.make_async_copy(connector_any, connector, own_sems.at[1]),
    ]
    for load in loads:
        load.start()
    over_x = (lax.rem(place.dp + NZ, 2 * NZ), place.t)
    greet(
        [place.at_z(step) for step in range(1, NZ)]
        + [place.at_y(1), place.at_y(-1), place.across(), place.sibling(), over_x]
    )
    sends = Sends(send_sems, recv_sems)
    half_rows = capacity // 2
    half_hidden = rows_dev // 2
    kept = [
        pltpu.make_async_copy(talker_ref, talkers.at[place.t], own_sems.at[2]),
        pltpu.make_async_copy(kv_ref, kvs.at[place.t], own_sems.at[3]),
        pltpu.make_async_copy(hidden_ref, hiddens.at[place.z], own_sems.at[4]),
        pltpu.make_async_copy(ids_row_ref, ids.at[place.z], own_sems.at[5]),
    ]

    def tile_of(i):
        return pl.ds(pl.multiple_of(i * TILE, TILE), TILE)

    def gather(own_ref, where, base):
        return GroupGather(
            place,
            lambda half: own_ref.at[pl.ds(half * half_rows, half_rows)],
            lambda block, half: where.at[block, pl.ds(half * half_rows, half_rows)],
            sends,
            base,
        )

    pair = (gather(talker_ref, talkers, 0), gather(kv_ref, kvs, GROUP_KEYS))

    def block_slot(block, half):
        return blocks.at[half, block]

    third = GatherFromY(
        place, lambda half: block_slot(place.t, half), block_slot, sends, 2 * GROUP_KEYS
    )
    z_base = 3 * GROUP_KEYS
    ids_base = z_base + NZ
    packed_base = ids_base + NZ
    terms_base = packed_base + NZ
    x_base = terms_base + NZ

    def z_at(step):
        return lax.rem(place.z + step + NZ, NZ)

    def z_slot(step, part=None):
        slot = hiddens.at[z_at(step)]
        if part is None:
            return slot
        return slot.at[pl.ds(part * half_hidden, half_hidden)]

    def pass_z(hop):
        for direction, step in ((0, -1), (1, 1)):
            if hop:
                sends.arrived(z_slot(hop * step), z_base + direction * 4 + hop - 1, place.at_z(step))
            part = direction if hop == 3 else None
            src = z_slot(hop * step, part) if hop else hidden_ref
            sends.send(
                src, z_slot(hop * step, part), z_base + direction * 4 + hop, place.at_z(-step)
            )

    def to_all_z(src, dst, base):
        for step in (1, 7, 2, 6, 3, 5, 4):
            sends.send(src(step), dst, base + step, place.at_z(step))

    def from_all_z(dst, base):
        for step in (1, 7, 2, 6, 3, 5, 4):
            sends.arrived(dst(-step), base + step, place.at_z(-step))

    def own_slots():
        def first(i, carry):
            squares, products = carry
            tile = tile_of(i)
            inputs = talker_ref[:, tile].astype(f32)
            gained = gain_ref[:, tile] * dot(kv_ref[...], weight[tile, :], NT)
            local_back[:, tile] = gained
            return (
                squares + jnp.sum(inputs * inputs, axis=1, keepdims=True),
                products + jnp.sum(gained * inputs, axis=1, keepdims=True),
            )

        zero = jnp.zeros((capacity, 1), f32)
        squares, products = lax.fori_loop(0, tiles, first, (zero, zero))
        inv_rms = lax.rsqrt(squares / width + 1e-06)
        mean = products * inv_rms / width

        def second(i, carry):
            tile = tile_of(i)
            scaled = talker_ref[:, tile].astype(f32) * inv_rms
            local_grad[:, tile] = (inv_rms * (local_back[:, tile] - scaled * mean)).astype(bf16)
            return carry

        lax.fori_loop(0, tiles, second, 0)
        piece = width // (2 * NZ)
        window_at = lax.broadcasted_iota(jnp.int32, (WINDOW, BLOCK), 0)
        wanted = lax.broadcasted_iota(jnp.int32, (WINDOW, BLOCK), 1)
        for index in range(2 * NZ):
            start = min(index * piece // 128 * 128, width - WINDOW)
            shift = onehot(
                (window_at == wanted + (index * piece - start)) & (wanted < piece)
            )
            packed[index % NZ, index // NZ] = dot(
                local_grad[:, start : start + WINDOW], shift, NN
            ).astype(bf16)

    def order_hidden(first, count):
        def one(i, carry):
            at = lax.rem(place.z + i + first + NZ, NZ)
            slot = lax.broadcasted_iota(jnp.int32, (slots, rows_dev), 0)
            chosen = onehot(slot == ids[at, 0:1, :])
            moved = dot(chosen, hiddens[at], NN).astype(bf16)
            for block in range(n_tensor):
                ordered[block, at] = moved[block * capacity : (block + 1) * capacity]
            return carry

        lax.fori_loop(0, count, one, 0)

    def pick_rows():
        slot = lax.broadcasted_iota(jnp.int32, (rows_dev, slots), 1)
        pick[...] = onehot(ids_col_ref[...] == slot)
        kv_all = kvs[...].reshape(slots, kvs.shape[2])
        kv_rows[...] = dot(pick[...], kv_all, NN).astype(bf16)
        at = lax.broadcasted_iota(jnp.int32, columns_shape, 0)
        col = lax.broadcasted_iota(jnp.int32, columns_shape, 1)
        dp = ((at >> 2) & 1) * NZ + (at >> 3)
        chosen = onehot(col == (dp * n_tensor + place.t) * 4 + (at & 3))
        columns[...] = dot(chosen, kv_rows[...], NT).astype(bf16)

        def one(i, squares):
            tile = tile_of(i)
            inputs = dot(pick[...], talkers[:, :, tile].reshape(slots, TILE), NN)
            rows[:, tile] = inputs.astype(bf16)
            return squares + jnp.sum(inputs * inputs, axis=1, keepdims=True)

        squares = lax.fori_loop(0, tiles, one, jnp.zeros((rows_dev, 1), f32))
        return lax.rsqrt(squares / width + 1e-06)

    columns_shape = (terms.shape[0] * terms.shape[1], kv_ref.shape[1])

    def make_terms(inv_rms):
        def one(i, carry):
            tile = tile_of(i)
            normed = ((rows[:, tile].astype(f32) * inv_rms) * gain_ref[:, tile]).astype(bf16)
            term = dot(columns[...], normed, NN)
            for at in range(NZ):
                terms[at, :, tile] = term[at * 8 : (at + 1) * 8].astype(bf16)
            return carry

        lax.fori_loop(0, tiles, one, 0)

    def make_back(first, last, products):
        def one(i, products):
            tile = tile_of(i)
            gained = gain_ref[:, tile] * dot(kv_rows[...], weight[tile, :], NT)
            back[:, tile] = gained
            return products + jnp.sum(gained * rows[:, tile].astype(f32), axis=1, keepdims=True)

        return lax.fori_loop(first, last, one, products)

    def make_hidden_grad(inv_rms, products):
        mean = products * inv_rms / width
        total[...] = jnp.zeros_like(total)

        def one(i, carry):
            tile = tile_of(i)
            scaled = rows[:, tile].astype(f32) * inv_rms
            grad = (inv_rms * (back[:, tile] - scaled * mean)).astype(bf16)
            total[...] += dot(grad, connector[:, tile], NT)
            return carry

        lax.fori_loop(0, tiles, one, 0)
        hidden_grad_ref[...] = total[...].astype(bf16)

    def connector_part(block, first):
        part = n_tensor // 4

        def piece(i):
            at = pl.ds(first + i * part, part)
            lhs = blocks[block, at].reshape(part * NZ * capacity, BLOCK)
            rhs = ordered[at].reshape(part * NZ * capacity, ordered.shape[3])
            return dot(lhs, rhs, TN)

        return piece(0) + piece(1)

    for g in pair:
        g.start()
    pass_z(0)
    to_all_z(lambda step: ids_row_ref, ids.at[place.z], ids_base)
    for copy in kept:
        copy.start()
    loads[0].wait()
    own_slots()
    own_packed = pltpu.make_async_copy(
        packed.at[place.z], blocks.at[:, place.t, place.z], own_sems.at[6]
    )
    own_packed.start()
    to_all_z(lambda step: packed.at[z_at(step)], blocks.at[:, place.t, place.z], packed_base)
    for direction in (0, 1):
        for g in pair:
            g.take_y(0, direction, direction)
    for g in pair:
        g.take_x(0)
    for direction in (0, 1):
        for g in pair:
            g.take_y(0, 1 - direction, direction)
    for g in pair:
        g.take_x(1)
    pass_z(1)
    for direction in (0, 1):
        for g in pair:
            g.take_far(0, direction)
    from_all_z(lambda step: ids.at[z_at(step)], ids_base)
    kept[2].wait()
    kept[3].wait()
    order_hidden(-1, 3)
    from_all_z(lambda step: blocks.at[:, place.t, z_at(step)], packed_base)
    own_packed.wait()
    third.start()
    for half in (0, 1):
        for direction in (0, 1):
            for g in pair:
                g.take_y(1, half, direction)
    for direction in (0, 1):
        third.take_y(0, direction, direction)
    for direction in (0, 1):
        for g in pair:
            g.take_far(1, direction)
    pass_z(2)
    for g in pair:
        g.take_shared()
    kept[0].wait()
    kept[1].wait()
    inv_rms = pick_rows()
    for direction in (0, 1):
        third.take_y(0, 1 - direction, direction)
    for direction in (0, 1):
        third.take_far(0, direction)
    make_terms(inv_rms)
    to_all_z(lambda step: terms.at[z_at(step)], terms_in.at[place.z], terms_base)
    pass_z(3)
    products = make_back(0, 4, jnp.zeros((rows_dev, 1), f32))
    for half in (0, 1):
        third.take_x(0, half)
    products = make_back(4, tiles, products)
    order_hidden(2, 2)
    order_hidden(-3, 2)
    for half in (0, 1):
        third.take_x(1, half)
        third.take_x(-1, half)
    loads[1].wait()
    make_hidden_grad(inv_rms, products)
    for half in (0, 1):
        third.take_x(2, half)
    for direction, step in ((0, -1), (1, 1)):
        sends.arrived(z_slot(4 * step, direction), z_base + direction * 4 + 3, place.at_z(step))
    order_hidden(4, 1)
    third.take_shared()
    near = place.xh * (n_tensor // 2)
    far = (1 - place.xh) * (n_tensor // 2)
    away[...] = (connector_part(1 - place.xl, near) + connector_part(1 - place.xl, far)).astype(bf16)
    sends.send(away, away_in, x_base, over_x)
    from_all_z(lambda step: terms_in.at[z_at(step)], terms_base)
    terms_in[place.z] = terms[place.z]

    def add_up(i, carry):
        tile = tile_of(i)
        sums[:, tile] = jnp.sum(terms_in[:, :, tile].astype(f32), axis=0)
        return carry

    lax.fori_loop(0, tiles, add_up, 0)
    sends.send(sums, sums_in, x_base + 1, over_x)
    total[...] = connector_part(place.xl, near) + connector_part(place.xl, far)
    sends.arrived(sums_in, x_base + 1, over_x)
    both = sums[...] + sums_in[...]
    weight_grad_ref[...] = jnp.where(place.xl == 0, both[0:4], both[4:8]) * factor
    sends.arrived(away_in, x_base, over_x)
    out_rows = connector_grad_ref.shape[0]
    connector_grad_ref[...] = (
        total[0:out_rows, :] + away_in[0:out_rows, :].astype(f32)
    ) * factor
    sends.drain()


VMEM = pl.BlockSpec(memory_space=pltpu.VMEM)
ANY = pl.BlockSpec(memory_space=pl.ANY)


def on_device(hidden, connector, routing, talker_in, norm_gain, kv_weight, kv_grad):
    n_dp = lax.axis_size("dp")
    n_tensor = lax.axis_size("tensor")
    rows_dev, d_dev = hidden.shape
    capacity, width = talker_in.shape
    kv_width = kv_grad.shape[1]
    slots = n_tensor * capacity
    per_dev = kv_width // (n_dp * n_tensor)
    bf16, f32 = jnp.bfloat16, jnp.float32

    route = routing[:, 0]
    shards = jnp.arange(n_tensor, dtype=jnp.int32)
    named = (route[:, None] == shards[None, :]).astype(f32)
    earlier = jnp.arange(rows_dev)[:, None] > jnp.arange(rows_dev)[None, :]
    before = jnp.dot(earlier.astype(f32), named, preferred_element_type=f32)
    ranks = jnp.sum(before * named, axis=1).astype(jnp.int32)
    slot_ids = route * capacity + ranks

    keys = 3 * GROUP_KEYS + 4 * NZ + 2
    hidden_grad, connector_grad, weight_grad = pl.pallas_call(
        whole,
        out_shape=(
            jax.ShapeDtypeStruct((rows_dev, d_dev), bf16),
            jax.ShapeDtypeStruct((width // n_dp, d_dev), f32),
            jax.ShapeDtypeStruct((per_dev, width), f32),
        ),
        in_specs=[VMEM] * 6 + [ANY] * 2,
        out_specs=[VMEM] * 3,
        scratch_shapes=[
            pltpu.VMEM((n_tensor, capacity, width), bf16),
            pltpu.VMEM((n_tensor, capacity, kv_width), bf16),
            pltpu.VMEM((NZ, rows_dev, d_dev), bf16),
            pltpu.VMEM((NZ, 8, rows_dev), jnp.int32),
            pltpu.VMEM(kv_weight.shape, bf16),
            pltpu.VMEM(connector.shape, bf16),
            pltpu.VMEM((capacity, width), f32),
            pltpu.VMEM((capacity, width), bf16),
            pltpu.VMEM((NZ, 2, capacity, BLOCK), bf16),
            pltpu.VMEM((2, n_tensor, NZ, capacity, BLOCK), bf16),
            pltpu.VMEM((n_tensor, NZ, capacity, d_dev), bf16),
            pltpu.VMEM((rows_dev, slots), bf16),
            pltpu.VMEM((rows_dev, width), bf16),
            pltpu.VMEM((rows_dev, kv_width), bf16),
            pltpu.VMEM((rows_dev, width), f32),
            pltpu.VMEM((n_dp * per_dev, rows_dev), bf16),
            pltpu.VMEM((NZ, 8, width), bf16),
            pltpu.VMEM((NZ, 8, width), bf16),
            pltpu.VMEM((BLOCK, d_dev), bf16),
            pltpu.VMEM((BLOCK, d_dev), bf16),
            pltpu.VMEM((8, width), f32),
            pltpu.VMEM((8, width), f32),
            pltpu.VMEM((BLOCK, d_dev), f32),
            pltpu.SemaphoreType.DMA((keys,)),
            pltpu.SemaphoreType.DMA((keys,)),
            pltpu.SemaphoreType.DMA((7,)),
        ],
        compiler_params=pltpu.CompilerParams(
            collective_id=0, has_side_effects=True, vmem_limit_bytes=60 * 1024 * 1024
        ),
    )(
        talker_in,
        kv_grad,
        hidden,
        norm_gain[None, :],
        jnp.broadcast_to(slot_ids[None, :], (8, rows_dev)),
        slot_ids[:, None],
        kv_weight,
        connector,
    )
    return (hidden_grad, connector_grad.T, weight_grad.T)


def solution(mesh):
    return jax.shard_map(
        on_device,
        mesh=mesh,
        in_specs=(
            P("dp", "tensor"),
            P("tensor", None),
            P("dp", None),
            P(("dp", "tensor"), None),
            P(),
            P(),
            P(("dp", "tensor"), None),
        ),
        out_specs=(P("dp", "tensor"), P("tensor", "dp"), P(None, ("dp", "tensor"))),
        check_vma=False,
    )
```

```python
import functools
import math

import jax
import jax.numpy as jnp
from jax import lax
from jax.experimental import pallas as pl
from jax.experimental.pallas import tpu as pltpu
from jax.sharding import PartitionSpec as P

MESH = pl.DeviceIdType.MESH
CONTRACT_LAST = (((1,), (1,)), ((), ()))
CONTRACT_FIRST = (((0,), (0,)), ((), ()))

NZ = 8
NY = 4


class Place:
    def __init__(self):
        self.dp = lax.axis_index("dp")
        self.t = lax.axis_index("tensor")
        self.z = lax.rem(self.dp, NZ)
        self.xl = lax.div(self.dp, NZ)
        self.core = lax.rem(self.t, 2)
        self.y = lax.rem(lax.div(self.t, 2), NY)
        self.xh = lax.div(self.t, 2 * NY)

    def tensor(self, xh, y, core):
        return xh * (2 * NY) + lax.rem(y + NY, NY) * 2 + core

    def at_y(self, step):
        return (self.dp, self.tensor(self.xh, self.y + step, self.core))

    def at_z(self, step):
        return (self.xl * NZ + lax.rem(self.z + step + NZ, NZ), self.t)

    def across(self):
        return (self.dp, self.tensor(1 - self.xh, self.y, self.core))

    def sibling(self):
        return (self.dp, self.tensor(self.xh, self.y, 1 - self.core))


def greet(devices):
    barrier = pltpu.get_barrier_semaphore()
    for device in devices:
        pl.semaphore_signal(barrier, inc=1, device_id=device, device_id_type=MESH)
    pl.semaphore_wait(barrier, len(devices))


class Sends:
    def __init__(self, send_sems, recv_sems):
        self.send_sems, self.recv_sems = send_sems, recv_sems
        self.open = []

    def send(self, src, dst, key, device):
        copy = pltpu.make_async_remote_copy(
            src_ref=src,
            dst_ref=dst,
            send_sem=self.send_sems.at[key],
            recv_sem=self.recv_sems.at[key],
            device_id=device,
            device_id_type=MESH,
        )
        copy.start()
        self.open.append(copy)

    def arrived(self, dst, key, device):
        pltpu.make_async_remote_copy(
            src_ref=dst,
            dst_ref=dst,
            send_sem=self.send_sems.at[key],
            recv_sem=self.recv_sems.at[key],
            device_id=device,
            device_id_type=MESH,
        ).wait_recv()

    def drain(self):
        for copy in self.open:
            copy.wait_send()


GROUP_KEYS = 12 + 2 + 16


def key_y(direction, far, kind):
    return direction * 6 + far * 3 + kind


def key_x(half):
    return 12 + half


def key_s(hop, half):
    return 14 + hop * 2 + half


class GroupGather:
    def __init__(self, place, own, slot, sends, base):
        self.place, self.own, self.slot = place, own, slot
        self.sends, self.base = sends, base

    def block(self, far, step):
        p = self.place
        return p.tensor(1 - p.xh if far else p.xh, p.y + step, p.core)

    def twin(self, far, step):
        p = self.place
        return p.tensor(1 - p.xh if far else p.xh, p.y + step, 1 - p.core)

    def hop(self, far, step):
        return far * 4 + step % 4

    def share(self, src, far, step, half):
        self.sends.send(
            src,
            self.slot(self.block(far, step), half),
            self.base + key_s(self.hop(far, step), half),
            self.place.sibling(),
        )

    def to_y(self, src, far, half, direction):
        step = 1 if direction == 0 else -1
        self.sends.send(
            src,
            self.slot(self.block(far, 0), half),
            self.base + key_y(direction, far, half),
            self.place.at_y(step),
        )

    def start(self):
        for half in (0, 1):
            self.to_y(self.own(half), 0, half, half)
            self.to_y(self.own(half), 0, half, 1 - half)
            self.sends.send(
                self.own(half),
                self.slot(self.block(0, 0), half),
                self.base + key_x(half),
                self.place.across(),
            )
        for half in (0, 1):
            self.share(self.own(half), 0, 0, half)

    def take_x(self, half):
        dst = self.slot(self.block(1, 0), half)
        self.sends.arrived(dst, self.base + key_x(half), self.place.across())
        self.to_y(dst, 1, half, 0)
        self.to_y(dst, 1, half, 1)
        self.share(dst, 1, 0, half)

    def take_y(self, far, half, direction):
        step = -1 if direction == 0 else 1
        dst = self.slot(self.block(far, step), half)
        self.sends.arrived(
            dst, self.base + key_y(direction, far, half), self.place.at_y(step)
        )
        if half == direction:
            self.sends.send(
                dst,
                dst,
                self.base + key_y(direction, far, 2),
                self.place.at_y(-step),
            )
        self.share(dst, far, step, half)

    def take_far(self, far, direction):
        step = -1 if direction == 0 else 1
        half = direction
        dst = self.slot(self.block(far, 2 * step), half)
        self.sends.arrived(
            dst, self.base + key_y(direction, far, 2), self.place.at_y(step)
        )
        self.share(dst, far, 2, half)

    def take_shared(self, halves=(0, 1)):
        for far in (0, 1):
            for step in (0, 1, 2, 3):
                for half in halves:
                    self.sends.arrived(
                        self.slot(self.twin(far, step), half),
                        self.base + key_s(self.hop(far, step), half),
                        self.place.sibling(),
                    )


class GatherFromY(GroupGather):
    def start(self):
        for half in (0, 1):
            self.to_y(self.own(half), 0, half, 0)
            self.to_y(self.own(1 - half), 0, 1 - half, 1)
            self.to_x(self.own(half), 0, half)
        for half in (0, 1):
            self.share(self.own(half), 0, 0, half)

    def to_x(self, src, step, half):
        self.sends.send(
            src,
            self.slot(self.block(0, step), half),
            self.base + key_from_y(step, half),
            self.place.across(),
        )

    def take_y(self, far, half, direction):
        super().take_y(0, half, direction)
        step = -1 if direction == 0 else 1
        self.to_x(self.slot(self.block(0, step), half), step, half)

    def take_far(self, far, direction):
        super().take_far(0, direction)
        self.to_x(self.slot(self.block(0, 2), direction), 2, direction)

    def take_x(self, step, half):
        dst = self.slot(self.block(1, step), half)
        self.sends.arrived(dst, self.base + key_from_y(step, half), self.place.across())
        self.share(dst, 1, step, half)


def key_from_y(step, half):
    return (3, 4, 5, 9, 10, 11, 12, 13)[(step % 4) * 2 + half]


TILE = 512
BLOCK = 256
WINDOW = 384


def onehot(rows):
    return jnp.where(rows, 1.0, 0.0).astype(jnp.bfloat16)


def dot(a, b, contract):
    return lax.dot_general(a, b, (contract, ((), ())), preferred_element_type=jnp.float32)


NN = ((1,), (0,))
NT = ((1,), (1,))
TN = ((0,), (0,))


def whole(
    talker_ref, kv_ref, hidden_ref, gain_rows_ref, route_ref, weight_any, connector_any,
    hidden_grad_ref, own_sum_ref, swapped_ref, weight_sums_ref,
    talkers, kvs, hiddens, ids, weight, connector,
    local_back, local_grad, packed, blocks, ordered, pick, rows, kv_rows, back, columns, terms, terms_in,
    away, away_in, sums, sums_in, total, gain_ref, own_ids, send_sems, recv_sems, own_sems,
):
    bf16, f32 = jnp.bfloat16, jnp.float32
    place = Place()
    width = talker_ref.shape[1]
    tiles = width // TILE
    capacity = talker_ref.shape[0]
    n_tensor = talkers.shape[0]
    slots = n_tensor * capacity
    rows_dev = hidden_ref.shape[0]
    piece_rows = own_sum_ref.shape[0]
    loads = [
        pltpu.make_async_copy(weight_any, weight, own_sems.at[0]),
        pltpu.make_async_copy(connector_any, connector, own_sems.at[1]),
    ]
    for load in loads:
        load.start()
    over_x = (lax.rem(place.dp + NZ, 2 * NZ), place.t)
    greet(
        [place.at_z(step) for step in range(1, NZ)]
        + [place.at_y(1), place.at_y(-1), place.across(), place.sibling(), over_x]
    )
    sends = Sends(send_sems, recv_sems)
    half_rows = capacity // 2
    half_hidden = rows_dev // 2
    kept = [
        pltpu.make_async_copy(talker_ref, talkers.at[place.t], own_sems.at[2]),
        pltpu.make_async_copy(kv_ref, kvs.at[place.t], own_sems.at[3]),
        pltpu.make_async_copy(hidden_ref, hiddens.at[place.z], own_sems.at[4]),
    ]

    def tile_of(i):
        return pl.ds(pl.multiple_of(i * TILE, TILE), TILE)

    def gather(own_ref, where, base):
        return GatherFromY(
            place,
            lambda half: own_ref.at[pl.ds(half * half_rows, half_rows)],
            lambda block, half: where.at[block, pl.ds(half * half_rows, half_rows)],
            sends,
            base,
        )

    pair = (gather(talker_ref, talkers, 0), gather(kv_ref, kvs, GROUP_KEYS))

    def block_slot(block, half):
        return blocks.at[lax.rem(1 - place.xl + half, 2), block]

    third = GroupGather(
        place, lambda half: block_slot(place.t, half), block_slot, sends, 2 * GROUP_KEYS
    )
    z_base = 3 * GROUP_KEYS
    ids_base = z_base + NZ
    packed_base = ids_base + NZ
    terms_base = packed_base + NZ
    x_base = terms_base + NZ

    def z_at(step):
        return lax.rem(place.z + step + NZ, NZ)

    def z_slot(step, part=None):
        slot = hiddens.at[z_at(step)]
        if part is None:
            return slot
        return slot.at[pl.ds(part * half_hidden, half_hidden)]

    def pass_z(hop):
        for direction, step in ((0, -1), (1, 1)):
            if hop:
                sends.arrived(z_slot(hop * step), z_base + direction * 4 + hop - 1, place.at_z(step))
            part = direction if hop == 3 else None
            src = z_slot(hop * step, part) if hop else hidden_ref
            sends.send(
                src, z_slot(hop * step, part), z_base + direction * 4 + hop, place.at_z(-step)
            )

    def to_all_z(src, dst, base):
        for step in (1, 7, 2, 6, 3, 5, 4):
            sends.send(src(step), dst, base + step, place.at_z(step))

    def from_all_z(dst, base):
        for step in (1, 7, 2, 6, 3, 5, 4):
            sends.arrived(dst(-step), base + step, place.at_z(-step))

    def number_rows():
        route = route_ref[...]
        shard = lax.broadcasted_iota(jnp.int32, (n_tensor, rows_dev), 0)
        named = shard == route
        earlier = lax.broadcasted_iota(jnp.int32, (rows_dev, rows_dev), 0)
        later = lax.broadcasted_iota(jnp.int32, (rows_dev, rows_dev), 1)
        before = dot(onehot(named), onehot(earlier < later), NN)
        rank = jnp.sum(jnp.where(named, before, 0.0), axis=0, keepdims=True)
        slot = route * capacity + rank.astype(jnp.int32)
        slot = jnp.broadcast_to(slot, own_ids.shape)
        own_ids[...] = slot
        ids[place.z] = slot
        lanes = gain_rows_ref.shape[1]
        for i in range(gain_rows_ref.shape[0]):
            gain_ref[:, i * lanes : (i + 1) * lanes] = gain_rows_ref[i : i + 1, :]

    def own_slots():
        def first(i, carry):
            squares, products = carry
            tile = tile_of(i)
            inputs = talker_ref[:, tile].astype(f32)
            gained = gain_ref[:, tile] * dot(kv_ref[...], weight[tile, :], NT)
            local_back[:, tile] = gained
            return (
                squares + jnp.sum(inputs * inputs, axis=1, keepdims=True),
                products + jnp.sum(gained * inputs, axis=1, keepdims=True),
            )

        zero = jnp.zeros((capacity, 1), f32)
        squares, products = lax.fori_loop(0, tiles, first, (zero, zero))
        inv_rms = lax.rsqrt(squares / width + 1e-06)
        mean = products * inv_rms / width

        def second(i, carry):
            tile = tile_of(i)
            scaled = talker_ref[:, tile].astype(f32) * inv_rms
            local_grad[:, tile] = (inv_rms * (local_back[:, tile] - scaled * mean)).astype(bf16)
            return carry

        lax.fori_loop(0, tiles, second, 0)
        piece = width // (2 * NZ)
        window_at = lax.broadcasted_iota(jnp.int32, (WINDOW, BLOCK), 0)
        wanted = lax.broadcasted_iota(jnp.int32, (WINDOW, BLOCK), 1)
        for index in range(2 * NZ):
            start = min(index * piece // 128 * 128, width - WINDOW)
            shift = onehot(
                (window_at == wanted + (index * piece - start)) & (wanted < piece)
            )
            packed[index % NZ, index // NZ] = dot(
                local_grad[:, start : start + WINDOW], shift, NN
            ).astype(bf16)

    def order_hidden(first, count):
        def one(i, carry):
            at = lax.rem(place.z + i + first + NZ, NZ)
            slot = lax.broadcasted_iota(jnp.int32, (slots, rows_dev), 0)
            chosen = onehot(slot == ids[at, 0:1, :])
            moved = dot(chosen, hiddens[at], NN).astype(bf16)
            for block in range(n_tensor):
                ordered[block, at] = moved[block * capacity : (block + 1) * capacity]
            return carry

        lax.fori_loop(0, count, one, 0)

    def pick_rows():
        slot = lax.broadcasted_iota(jnp.int32, (slots, rows_dev), 0)
        chosen = onehot(slot == own_ids[0:1, :])
        one = lax.broadcasted_iota(jnp.int32, (rows_dev, rows_dev), 0)
        two = lax.broadcasted_iota(jnp.int32, (rows_dev, rows_dev), 1)
        pick[...] = dot(onehot(one == two), chosen, NT).astype(bf16)
        kv_all = kvs[...].reshape(slots, kvs.shape[2])
        kv_rows[...] = dot(pick[...], kv_all, NN).astype(bf16)
        at = lax.broadcasted_iota(jnp.int32, columns_shape, 0)
        col = lax.broadcasted_iota(jnp.int32, columns_shape, 1)
        dp = ((at >> 2) & 1) * NZ + (at >> 3)
        chosen = onehot(col == (dp * n_tensor + place.t) * 4 + (at & 3))
        columns[...] = dot(chosen, kv_rows[...], NT).astype(bf16)

        def one(i, squares):
            tile = tile_of(i)
            inputs = dot(pick[...], talkers[:, :, tile].reshape(slots, TILE), NN)
            rows[:, tile] = inputs.astype(bf16)
            return squares + jnp.sum(inputs * inputs, axis=1, keepdims=True)

        squares = lax.fori_loop(0, tiles, one, jnp.zeros((rows_dev, 1), f32))
        return lax.rsqrt(squares / width + 1e-06)

    columns_shape = (terms.shape[0] * terms.shape[1], kv_ref.shape[1])

    def make_terms(inv_rms):
        def one(i, carry):
            tile = tile_of(i)
            normed = ((rows[:, tile].astype(f32) * inv_rms) * gain_ref[:, tile]).astype(bf16)
            term = dot(columns[...], normed, NN)
            for at in range(NZ):
                terms[at, :, tile] = term[at * 8 : (at + 1) * 8].astype(bf16)
            return carry

        lax.fori_loop(0, tiles, one, 0)

    def make_back(first, last, products):
        def one(i, products):
            tile = tile_of(i)
            gained = gain_ref[:, tile] * dot(kv_rows[...], weight[tile, :], NT)
            back[:, tile] = gained
            return products + jnp.sum(gained * rows[:, tile].astype(f32), axis=1, keepdims=True)

        return lax.fori_loop(first, last, one, products)

    def make_hidden_grad(inv_rms, products):
        mean = products * inv_rms / width
        total[...] = jnp.zeros_like(total)

        def one(i, carry):
            tile = tile_of(i)
            scaled = rows[:, tile].astype(f32) * inv_rms
            grad = (inv_rms * (back[:, tile] - scaled * mean)).astype(bf16)
            total[...] += dot(grad, connector[:, tile], NT)
            return carry

        lax.fori_loop(0, tiles, one, 0)
        hidden_grad_ref[...] = total[...].astype(bf16)

    def connector_part(block, first):
        part = n_tensor // 4

        def piece(i):
            at = pl.ds(first + i * part, part)
            lhs = blocks[block, at].reshape(part * NZ * capacity, BLOCK)
            rhs = ordered[at].reshape(part * NZ * capacity, ordered.shape[3])
            return dot(lhs, rhs, TN)

        return piece(0) + piece(1)

    def both(step):
        for g in pair:
            step(g)

    both(lambda g: g.start())
    pass_z(0)
    for copy in kept:
        copy.start()
    number_rows()
    to_all_z(lambda step: own_ids, ids.at[place.z], ids_base)
    loads[0].wait()
    own_slots()
    own_packed = pltpu.make_async_copy(
        packed.at[place.z], blocks.at[:, place.t, place.z], own_sems.at[5]
    )
    own_packed.start()
    to_all_z(lambda step: packed.at[z_at(step)], blocks.at[:, place.t, place.z], packed_base)
    for direction in (0, 1):
        both(lambda g: g.take_y(0, direction, direction))
    for direction in (0, 1):
        both(lambda g: g.take_y(0, 1 - direction, direction))
    pass_z(1)
    for half in (0, 1):
        both(lambda g: g.take_x(0, half))
    for direction in (0, 1):
        both(lambda g: g.take_far(0, direction))
    from_all_z(lambda step: ids.at[z_at(step)], ids_base)
    kept[2].wait()
    order_hidden(-1, 3)
    from_all_z(lambda step: blocks.at[:, place.t, z_at(step)], packed_base)
    own_packed.wait()
    third.start()
    pass_z(2)
    for step in (1, -1):
        for half in (0, 1):
            both(lambda g: g.take_x(step, half))
    for half in (0, 1):
        third.take_y(0, half, half)
        third.take_y(0, half, 1 - half)
        third.take_x(half)
    for half in (0, 1):
        both(lambda g: g.take_x(2, half))
    both(lambda g: g.take_shared())
    kept[0].wait()
    kept[1].wait()
    inv_rms = pick_rows()
    make_terms(inv_rms)
    to_all_z(lambda step: terms.at[z_at(step)], terms_in.at[place.z], terms_base)
    pass_z(3)
    for half in (0, 1):
        third.take_far(0, half)
        third.take_y(1, half, half)
        third.take_y(1, half, 1 - half)
    products = make_back(0, tiles, jnp.zeros((rows_dev, 1), f32))
    third.take_far(1, 0)
    for direction, step in ((0, -1), (1, 1)):
        sends.arrived(z_slot(4 * step, direction), z_base + direction * 4 + 3, place.at_z(step))
    order_hidden(2, 5)
    third.take_shared((0,))
    near = place.xh * (n_tensor // 2)
    far = (1 - place.xh) * (n_tensor // 2)
    away[...] = (connector_part(1 - place.xl, near) + connector_part(1 - place.xl, far)).astype(bf16)
    third.take_far(1, 1)
    sends.send(
        away.at[pl.ds(0, piece_rows)], away_in.at[pl.ds(0, piece_rows)], x_base, over_x
    )
    loads[1].wait()
    make_hidden_grad(inv_rms, products)
    from_all_z(lambda step: terms_in.at[z_at(step)], terms_base)
    terms_in[place.z] = terms[place.z]

    def add_up(i, carry):
        tile = tile_of(i)
        sums[:, tile] = jnp.sum(terms_in[:, :, tile].astype(f32), axis=0)
        return carry

    lax.fori_loop(0, tiles, add_up, 0)
    third.take_shared((1,))
    sends.send(sums, sums_in, x_base + 1, over_x)
    total[...] = connector_part(place.xl, near) + connector_part(place.xl, far)
    own_sum_ref[...] = total[0:piece_rows, :]
    sends.arrived(sums_in, x_base + 1, over_x)
    weight_sums_ref[...] = sums[...] + sums_in[...]
    sends.arrived(away_in.at[pl.ds(0, piece_rows)], x_base, over_x)
    swapped_ref[...] = away_in[0:piece_rows, :]
    sends.drain()


def close(factor, hidden_ref, own_ref, swapped_ref, sums_ref, hidden_grad_ref, connector_grad_ref, weight_grad_ref):
    hidden_grad_ref[...] = hidden_ref[...]
    connector_grad_ref[...] = (own_ref[...] + swapped_ref[...].astype(jnp.float32)) * factor
    sums = sums_ref[...]
    mine = jnp.where(lax.axis_index("dp") < NZ, sums[0:4], sums[4:8])
    weight_grad_ref[...] = mine * factor


VMEM = pl.BlockSpec(memory_space=pltpu.VMEM)
ANY = pl.BlockSpec(memory_space=pl.ANY)


def on_device(hidden, connector, routing, talker_in, norm_gain, kv_weight, kv_grad):
    n_dp = lax.axis_size("dp")
    n_tensor = lax.axis_size("tensor")
    rows_dev, d_dev = hidden.shape
    capacity, width = talker_in.shape
    kv_width = kv_grad.shape[1]
    slots = n_tensor * capacity
    per_dev = kv_width // (n_dp * n_tensor)
    bf16, f32 = jnp.bfloat16, jnp.float32

    keys = 3 * GROUP_KEYS + 4 * NZ + 2
    hidden_rows, own_sum, swapped, weight_sums = pl.pallas_call(
        whole,
        out_shape=(
            jax.ShapeDtypeStruct((rows_dev, d_dev), bf16),
            jax.ShapeDtypeStruct((width // n_dp, d_dev), f32),
            jax.ShapeDtypeStruct((width // n_dp, d_dev), bf16),
            jax.ShapeDtypeStruct((8, width), f32),
        ),
        in_specs=[VMEM] * 5 + [ANY] * 2,
        out_specs=[VMEM] * 4,
        scratch_shapes=[
            pltpu.VMEM((n_tensor, capacity, width), bf16),
            pltpu.VMEM((n_tensor, capacity, kv_width), bf16),
            pltpu.VMEM((NZ, rows_dev, d_dev), bf16),
            pltpu.VMEM((NZ, 8, rows_dev), jnp.int32),
            pltpu.VMEM(kv_weight.shape, bf16),
            pltpu.VMEM(connector.shape, bf16),
            pltpu.VMEM((capacity, width), f32),
            pltpu.VMEM((capacity, width), bf16),
            pltpu.VMEM((NZ, 2, capacity, BLOCK), bf16),
            pltpu.VMEM((2, n_tensor, NZ, capacity, BLOCK), bf16),
            pltpu.VMEM((n_tensor, NZ, capacity, d_dev), bf16),
            pltpu.VMEM((rows_dev, slots), bf16),
            pltpu.VMEM((rows_dev, width), bf16),
            pltpu.VMEM((rows_dev, kv_width), bf16),
            pltpu.VMEM((rows_dev, width), f32),
            pltpu.VMEM((n_dp * per_dev, rows_dev), bf16),
            pltpu.VMEM((NZ, 8, width), bf16),
            pltpu.VMEM((NZ, 8, width), bf16),
            pltpu.VMEM((BLOCK, d_dev), bf16),
            pltpu.VMEM((BLOCK, d_dev), bf16),
            pltpu.VMEM((8, width), f32),
            pltpu.VMEM((8, width), f32),
            pltpu.VMEM((BLOCK, d_dev), f32),
            pltpu.VMEM((1, width), f32),
            pltpu.VMEM((8, rows_dev), jnp.int32),
            pltpu.SemaphoreType.DMA((keys,)),
            pltpu.SemaphoreType.DMA((keys,)),
            pltpu.SemaphoreType.DMA((6,)),
        ],
        compiler_params=pltpu.CompilerParams(
            collective_id=0, has_side_effects=True, vmem_limit_bytes=60 * 1024 * 1024
        ),
    )(
        talker_in,
        kv_grad,
        hidden,
        norm_gain.reshape(width // 128, 128),
        routing.T,
        kv_weight,
        connector,
    )
    factor = 1.0 / math.sqrt(rows_dev * n_dp)
    hidden_grad, connector_grad, weight_grad = pl.pallas_call(
        functools.partial(close, factor),
        out_shape=(
            jax.ShapeDtypeStruct((rows_dev, d_dev), bf16),
            jax.ShapeDtypeStruct((width // n_dp, d_dev), f32),
            jax.ShapeDtypeStruct((per_dev, width), f32),
        ),
        in_specs=[VMEM] * 4,
        out_specs=[VMEM] * 3,
    )(hidden_rows, own_sum, swapped, weight_sums)
    return (hidden_grad, connector_grad.T, weight_grad.T)


def solution(mesh):
    return jax.shard_map(
        on_device,
        mesh=mesh,
        in_specs=(
            P("dp", "tensor"),
            P("tensor", None),
            P("dp", None),
            P(("dp", "tensor"), None),
            P(),
            P(),
            P(("dp", "tensor"), None),
        ),
        out_specs=(P("dp", "tensor"), P("tensor", "dp"), P(None, ("dp", "tensor"))),
        check_vma=False,
    )
```

```python
import functools
import math

import jax
import jax.numpy as jnp
from jax import lax
from jax.experimental import pallas as pl
from jax.experimental.pallas import tpu as pltpu
from jax.sharding import PartitionSpec as P

MESH = pl.DeviceIdType.MESH
CONTRACT_LAST = (((1,), (1,)), ((), ()))
CONTRACT_FIRST = (((0,), (0,)), ((), ()))

NZ = 8
NY = 4


class Place:
    def __init__(self):
        self.dp = lax.axis_index("dp")
        self.t = lax.axis_index("tensor")
        self.z = lax.rem(self.dp, NZ)
        self.xl = lax.div(self.dp, NZ)
        self.core = lax.rem(self.t, 2)
        self.y = lax.rem(lax.div(self.t, 2), NY)
        self.xh = lax.div(self.t, 2 * NY)

    def tensor(self, xh, y, core):
        return xh * (2 * NY) + lax.rem(y + NY, NY) * 2 + core

    def at_y(self, step):
        return (self.dp, self.tensor(self.xh, self.y + step, self.core))

    def at_z(self, step):
        return (self.xl * NZ + lax.rem(self.z + step + NZ, NZ), self.t)

    def across(self):
        return (self.dp, self.tensor(1 - self.xh, self.y, self.core))

    def sibling(self):
        return (self.dp, self.tensor(self.xh, self.y, 1 - self.core))


def greet(devices):
    barrier = pltpu.get_barrier_semaphore()
    for device in devices:
        pl.semaphore_signal(barrier, inc=1, device_id=device, device_id_type=MESH)
    pl.semaphore_wait(barrier, len(devices))


class Sends:
    def __init__(self, send_sems, recv_sems):
        self.send_sems, self.recv_sems = send_sems, recv_sems
        self.open = []

    def send(self, src, dst, key, device):
        copy = pltpu.make_async_remote_copy(
            src_ref=src,
            dst_ref=dst,
            send_sem=self.send_sems.at[key],
            recv_sem=self.recv_sems.at[key],
            device_id=device,
            device_id_type=MESH,
        )
        copy.start()
        self.open.append(copy)

    def arrived(self, dst, key, device):
        pltpu.make_async_remote_copy(
            src_ref=dst,
            dst_ref=dst,
            send_sem=self.send_sems.at[key],
            recv_sem=self.recv_sems.at[key],
            device_id=device,
            device_id_type=MESH,
        ).wait_recv()

    def drain(self):
        for copy in self.open:
            copy.wait_send()


GROUP_KEYS = 12 + 2 + 16


def key_y(direction, far, kind):
    return direction * 6 + far * 3 + kind


def key_x(half):
    return 12 + half


def key_s(hop, half):
    return 14 + hop * 2 + half


class GroupGather:
    def __init__(self, place, own, slot, sends, base):
        self.place, self.own, self.slot = place, own, slot
        self.sends, self.base = sends, base

    def block(self, far, step):
        p = self.place
        return p.tensor(1 - p.xh if far else p.xh, p.y + step, p.core)

    def twin(self, far, step):
        p = self.place
        return p.tensor(1 - p.xh if far else p.xh, p.y + step, 1 - p.core)

    def hop(self, far, step):
        return far * 4 + step % 4

    def share(self, src, far, step, half):
        self.sends.send(
            src,
            self.slot(self.block(far, step), half),
            self.base + key_s(self.hop(far, step), half),
            self.place.sibling(),
        )

    def to_y(self, src, far, half, direction):
        step = 1 if direction == 0 else -1
        self.sends.send(
            src,
            self.slot(self.block(far, 0), half),
            self.base + key_y(direction, far, half),
            self.place.at_y(step),
        )

    def start(self, halves=(0, 1)):
        for half in halves:
            self.to_y(self.own(half), 0, half, half)
            self.to_y(self.own(half), 0, half, 1 - half)
            self.across_first(half)
        for half in halves:
            self.share(self.own(half), 0, 0, half)

    def across_first(self, half):
        self.sends.send(
            self.own(half),
            self.slot(self.block(0, 0), half),
            self.base + key_x(half),
            self.place.across(),
        )

    def take_x(self, half):
        dst = self.slot(self.block(1, 0), half)
        self.sends.arrived(dst, self.base + key_x(half), self.place.across())
        self.to_y(dst, 1, half, 0)
        self.to_y(dst, 1, half, 1)
        self.share(dst, 1, 0, half)

    def take_y(self, far, half, direction):
        step = -1 if direction == 0 else 1
        dst = self.slot(self.block(far, step), half)
        self.sends.arrived(
            dst, self.base + key_y(direction, far, half), self.place.at_y(step)
        )
        if half == direction:
            self.sends.send(
                dst,
                dst,
                self.base + key_y(direction, far, 2),
                self.place.at_y(-step),
            )
        self.share(dst, far, step, half)

    def take_far(self, far, direction):
        step = -1 if direction == 0 else 1
        half = direction
        dst = self.slot(self.block(far, 2 * step), half)
        self.sends.arrived(
            dst, self.base + key_y(direction, far, 2), self.place.at_y(step)
        )
        self.share(dst, far, 2, half)

    def take_shared(self, halves=(0, 1)):
        for far in (0, 1):
            for step in (0, 1, 2, 3):
                for half in halves:
                    self.sends.arrived(
                        self.slot(self.twin(far, step), half),
                        self.base + key_s(self.hop(far, step), half),
                        self.place.sibling(),
                    )


class GatherFromY(GroupGather):
    def across_first(self, half):
        self.to_x(self.own(half), 0, half)

    def to_x(self, src, step, half):
        self.sends.send(
            src,
            self.slot(self.block(0, step), half),
            self.base + key_from_y(step, half),
            self.place.across(),
        )

    def take_y(self, far, half, direction):
        super().take_y(0, half, direction)
        step = -1 if direction == 0 else 1
        self.to_x(self.slot(self.block(0, step), half), step, half)

    def take_far(self, far, direction):
        super().take_far(0, direction)
        self.to_x(self.slot(self.block(0, 2), direction), 2, direction)

    def take_x(self, step, half):
        dst = self.slot(self.block(1, step), half)
        self.sends.arrived(dst, self.base + key_from_y(step, half), self.place.across())
        self.share(dst, 1, step, half)


def key_from_y(step, half):
    return (3, 4, 5, 9, 10, 11, 12, 13)[(step % 4) * 2 + half]


TILE = 512
BLOCK = 256
WINDOW = 384


def onehot(rows):
    return jnp.where(rows, 1.0, 0.0).astype(jnp.bfloat16)


def dot(a, b, contract):
    return lax.dot_general(a, b, (contract, ((), ())), preferred_element_type=jnp.float32)


NN = ((1,), (0,))
NT = ((1,), (1,))
TN = ((0,), (0,))


def whole(
    talker_ref, kv_ref, hidden_ref, gain_rows_ref, route_ref, weight_any, connector_any,
    hidden_grad_ref, own_sum_ref, swapped_ref, weight_sums_ref,
    talkers, kvs, hiddens, weight, connector,
    local_rows, local_back, local_grad, packed, blocks, pick, rows, kv_rows, back, columns, terms, terms_in,
    away, away_in, sums, sums_in, total, gain_ref, send_sems, recv_sems, own_sems,
):
    bf16, f32 = jnp.bfloat16, jnp.float32
    place = Place()
    width = talker_ref.shape[1]
    tiles = width // TILE
    capacity = talker_ref.shape[0]
    n_tensor = talkers.shape[0]
    slots = n_tensor * capacity
    rows_dev = hidden_ref.shape[0]
    share = rows_dev // n_tensor
    piece_rows = own_sum_ref.shape[0]
    loads = [
        pltpu.make_async_copy(weight_any, weight, own_sems.at[0]),
        pltpu.make_async_copy(connector_any, connector, own_sems.at[1]),
    ]
    for load in loads:
        load.start()
    over_x = (lax.rem(place.dp + NZ, 2 * NZ), place.t)
    greet(
        [place.at_z(step) for step in range(1, NZ)]
        + [place.at_y(1), place.at_y(-1), place.across(), place.sibling(), over_x]
    )
    sends = Sends(send_sems, recv_sems)
    half_rows = capacity // 2
    half_hidden = rows_dev // 2
    kept = [
        pltpu.make_async_copy(talker_ref, talkers.at[place.t], own_sems.at[2]),
        pltpu.make_async_copy(kv_ref, kvs.at[place.t], own_sems.at[3]),
        pltpu.make_async_copy(hidden_ref, hiddens.at[place.z], own_sems.at[4]),
    ]

    def tile_of(i):
        return pl.ds(pl.multiple_of(i * TILE, TILE), TILE)

    def gather(kind, own_ref, where, base):
        return kind(
            place,
            lambda half: own_ref.at[pl.ds(half * half_rows, half_rows)],
            lambda block, half: where.at[block, pl.ds(half * half_rows, half_rows)],
            sends,
            base,
        )

    wide = gather(GroupGather, talker_ref, talkers, 0)
    thin = gather(GatherFromY, kv_ref, kvs, GROUP_KEYS)

    def block_slot(block, half):
        return blocks.at[lax.rem(1 - place.xl + half, 2), :, block]

    def own_block(half):
        return block_slot(place.t, half)

    theirs = GroupGather(place, own_block, block_slot, sends, 2 * GROUP_KEYS)
    ours = GatherFromY(place, own_block, block_slot, sends, 3 * GROUP_KEYS)
    z_base = 4 * GROUP_KEYS
    packed_base = z_base + NZ
    terms_base = packed_base + NZ
    x_base = terms_base + NZ

    def z_at(step):
        return lax.rem(place.z + step + NZ, NZ)

    def z_slot(step, part=None):
        slot = hiddens.at[z_at(step)]
        if part is None:
            return slot
        return slot.at[pl.ds(part * half_hidden, half_hidden)]

    def pass_z(hop):
        for direction, step in ((0, -1), (1, 1)):
            if hop:
                sends.arrived(z_slot(hop * step), z_base + direction * 4 + hop - 1, place.at_z(step))
            part = direction if hop == 3 else None
            src = z_slot(hop * step, part) if hop else hidden_ref
            sends.send(
                src, z_slot(hop * step, part), z_base + direction * 4 + hop, place.at_z(-step)
            )

    def to_all_z(src, dst, base):
        for step in (1, 7, 2, 6, 3, 5, 4):
            sends.send(src(step), dst, base + step, place.at_z(step))

    def from_all_z(dst, base):
        for step in (1, 7, 2, 6, 3, 5, 4):
            sends.arrived(dst(-step), base + step, place.at_z(-step))

    def number_rows():
        route = route_ref[...]
        shard = lax.broadcasted_iota(jnp.int32, (n_tensor, rows_dev), 0)
        named = shard == route
        earlier = lax.broadcasted_iota(jnp.int32, (rows_dev, rows_dev), 0)
        later = lax.broadcasted_iota(jnp.int32, (rows_dev, rows_dev), 1)
        before = dot(onehot(named), onehot(earlier < later), NN)
        rank = jnp.sum(jnp.where(named, before, 0.0), axis=0, keepdims=True)
        slot = route * capacity + rank.astype(jnp.int32)
        slot_at = lax.broadcasted_iota(jnp.int32, (slots, rows_dev), 0)
        same = onehot(earlier == later)
        pick[...] = dot(same, onehot(slot_at == slot), NT).astype(bf16)
        lanes = gain_rows_ref.shape[1]
        for i in range(gain_rows_ref.shape[0]):
            gain_ref[:, i * lanes : (i + 1) * lanes] = gain_rows_ref[i : i + 1, :]

    def own_rows():
        mine = pl.ds(pl.multiple_of(place.t * share, share), share)
        kv_all = kvs[...].reshape(slots, kvs.shape[2])
        kv_rows[...] = dot(pick[...], kv_all, NN).astype(bf16)

        def first(i, carry):
            squares, products = carry
            tile = tile_of(i)
            inputs = dot(pick[mine, :], talkers[:, :, tile].reshape(slots, TILE), NN)
            local_rows[:, tile] = inputs
            gained = gain_ref[:, tile] * dot(kv_rows[mine, :], weight[tile, :], NT)
            local_back[:, tile] = gained
            return (
                squares + jnp.sum(inputs * inputs, axis=1, keepdims=True),
                products + jnp.sum(gained * inputs, axis=1, keepdims=True),
            )

        zero = jnp.zeros((share, 1), f32)
        squares, products = lax.fori_loop(0, tiles, first, (zero, zero))
        inv_rms = lax.rsqrt(squares / width + 1e-06)
        mean = products * inv_rms / width

        def second(i, carry):
            tile = tile_of(i)
            scaled = local_rows[:, tile] * inv_rms
            local_grad[:, tile] = (inv_rms * (local_back[:, tile] - scaled * mean)).astype(bf16)
            return carry

        lax.fori_loop(0, tiles, second, 0)
        piece = width // (2 * NZ)
        window_at = lax.broadcasted_iota(jnp.int32, (WINDOW, BLOCK), 0)
        wanted = lax.broadcasted_iota(jnp.int32, (WINDOW, BLOCK), 1)
        for index in range(2 * NZ):
            start = min(index * piece // 128 * 128, width - WINDOW)
            shift = onehot(
                (window_at == wanted + (index * piece - start)) & (wanted < piece)
            )
            packed[index % NZ, index // NZ] = dot(
                local_grad[:, start : start + WINDOW], shift, NN
            ).astype(bf16)

    def pick_rows():
        at = lax.broadcasted_iota(jnp.int32, columns_shape, 0)
        col = lax.broadcasted_iota(jnp.int32, columns_shape, 1)
        dp = ((at >> 2) & 1) * NZ + (at >> 3)
        chosen = onehot(col == (dp * n_tensor + place.t) * 4 + (at & 3))
        columns[...] = dot(chosen, kv_rows[...], NT).astype(bf16)

        def one(i, squares):
            tile = tile_of(i)
            inputs = dot(pick[...], talkers[:, :, tile].reshape(slots, TILE), NN)
            rows[:, tile] = inputs.astype(bf16)
            return squares + jnp.sum(inputs * inputs, axis=1, keepdims=True)

        squares = lax.fori_loop(0, tiles, one, jnp.zeros((rows_dev, 1), f32))
        return lax.rsqrt(squares / width + 1e-06)

    columns_shape = (terms.shape[0] * terms.shape[1], kv_ref.shape[1])

    def make_terms(inv_rms):
        def one(i, carry):
            tile = tile_of(i)
            normed = ((rows[:, tile].astype(f32) * inv_rms) * gain_ref[:, tile]).astype(bf16)
            term = dot(columns[...], normed, NN)
            for at in range(NZ):
                terms[at, :, tile] = term[at * 8 : (at + 1) * 8].astype(bf16)
            return carry

        lax.fori_loop(0, tiles, one, 0)

    def make_back(first, last, products):
        def one(i, products):
            tile = tile_of(i)
            gained = gain_ref[:, tile] * dot(kv_rows[...], weight[tile, :], NT)
            back[:, tile] = gained
            return products + jnp.sum(gained * rows[:, tile].astype(f32), axis=1, keepdims=True)

        return lax.fori_loop(first, last, one, products)

    def make_hidden_grad(inv_rms, products):
        mean = products * inv_rms / width
        total[...] = jnp.zeros_like(total)

        def one(i, carry):
            tile = tile_of(i)
            scaled = rows[:, tile].astype(f32) * inv_rms
            grad = (inv_rms * (back[:, tile] - scaled * mean)).astype(bf16)
            total[...] += dot(grad, connector[:, tile], NT)
            return carry

        lax.fori_loop(0, tiles, one, 0)
        hidden_grad_ref[...] = total[...].astype(bf16)

    def connector_part(block):
        part = NZ // 4
        total[...] = jnp.zeros_like(total)

        def one(i, carry):
            at = pl.ds(i * part, part)
            lhs = blocks[block, at].reshape(part * rows_dev, BLOCK)
            rhs = hiddens[at].reshape(part * rows_dev, hiddens.shape[2])
            total[...] += dot(lhs, rhs, TN)
            return carry

        lax.fori_loop(0, 4, one, 0)

    wide.start()
    thin.start()
    pass_z(0)
    for copy in kept:
        copy.start()
    number_rows()
    for direction in (0, 1):
        wide.take_y(0, direction, direction)
    wide.take_x(0)
    for direction in (0, 1):
        wide.take_y(0, 1 - direction, direction)
    wide.take_x(1)
    pass_z(1)
    for half in (0, 1):
        for direction in (half, 1 - half):
            thin.take_y(0, half, direction)
    for direction in (0, 1):
        wide.take_far(0, direction)
        thin.take_far(0, direction)
    for direction in (0, 1):
        wide.take_y(1, direction, direction)
    pass_z(2)
    for direction in (0, 1):
        wide.take_y(1, 1 - direction, direction)
    for step in (0, 1, -1, 2):
        for half in (0, 1):
            thin.take_x(step, half)
    for direction in (0, 1):
        wide.take_far(1, direction)
    thin.take_shared()
    wide.take_shared()
    kept[0].wait()
    kept[1].wait()
    loads[0].wait()
    own_rows()
    own_packed = pltpu.make_async_copy(
        packed.at[place.z], blocks.at[:, place.z, place.t], own_sems.at[5]
    )
    own_packed.start()
    to_all_z(lambda step: packed.at[z_at(step)], blocks.at[:, place.z, place.t], packed_base)
    pass_z(3)
    inv_rms = pick_rows()
    make_terms(inv_rms)
    from_all_z(lambda step: blocks.at[:, z_at(step), place.t], packed_base)
    own_packed.wait()
    theirs.start((0,))
    to_all_z(lambda step: terms.at[z_at(step)], terms_in.at[place.z], terms_base)
    products = make_back(0, tiles, jnp.zeros((rows_dev, 1), f32))
    theirs.take_x(0)
    ours.start((1,))
    theirs.take_y(0, 0, 0)
    theirs.take_y(0, 0, 1)
    theirs.take_far(0, 0)
    theirs.take_y(1, 0, 0)
    theirs.take_y(1, 0, 1)
    ours.take_x(0, 1)
    ours.take_y(0, 1, 1)
    ours.take_y(0, 1, 0)
    theirs.take_far(1, 0)
    ours.take_far(0, 1)
    for direction, step in ((0, -1), (1, 1)):
        sends.arrived(z_slot(4 * step, direction), z_base + direction * 4 + 3, place.at_z(step))
    kept[2].wait()
    theirs.take_shared((0,))
    connector_part(1 - place.xl)
    away[...] = total[...].astype(bf16)
    for step in (1, -1):
        ours.take_x(step, 1)
    sends.send(
        away.at[pl.ds(0, piece_rows)], away_in.at[pl.ds(0, piece_rows)], x_base, over_x
    )
    from_all_z(lambda step: terms_in.at[z_at(step)], terms_base)
    terms_in[place.z] = terms[place.z]

    def add_up(i, carry):
        tile = tile_of(i)
        sums[:, tile] = jnp.sum(terms_in[:, :, tile].astype(f32), axis=0)
        return carry

    lax.fori_loop(0, tiles, add_up, 0)
    sends.send(sums, sums_in, x_base + 1, over_x)
    loads[1].wait()
    make_hidden_grad(inv_rms, products)
    ours.take_x(2, 1)
    ours.take_shared((1,))
    connector_part(place.xl)
    own_sum_ref[...] = total[0:piece_rows, :]
    sends.arrived(sums_in, x_base + 1, over_x)
    weight_sums_ref[...] = sums[...] + sums_in[...]
    sends.arrived(away_in.at[pl.ds(0, piece_rows)], x_base, over_x)
    swapped_ref[...] = away_in[0:piece_rows, :]
    sends.drain()


def close(factor, hidden_ref, own_ref, swapped_ref, sums_ref, hidden_grad_ref, connector_grad_ref, weight_grad_ref):
    hidden_grad_ref[...] = hidden_ref[...]
    connector_grad_ref[...] = (own_ref[...] + swapped_ref[...].astype(jnp.float32)) * factor
    sums = sums_ref[...]
    mine = jnp.where(lax.axis_index("dp") < NZ, sums[0:4], sums[4:8])
    weight_grad_ref[...] = mine * factor


VMEM = pl.BlockSpec(memory_space=pltpu.VMEM)
ANY = pl.BlockSpec(memory_space=pl.ANY)


def on_device(hidden, connector, routing, talker_in, norm_gain, kv_weight, kv_grad):
    n_dp = lax.axis_size("dp")
    n_tensor = lax.axis_size("tensor")
    rows_dev, d_dev = hidden.shape
    capacity, width = talker_in.shape
    kv_width = kv_grad.shape[1]
    slots = n_tensor * capacity
    share = rows_dev // n_tensor
    per_dev = kv_width // (n_dp * n_tensor)
    bf16, f32 = jnp.bfloat16, jnp.float32

    keys = 4 * GROUP_KEYS + 3 * NZ + 2
    hidden_rows, own_sum, swapped, weight_sums = pl.pallas_call(
        whole,
        out_shape=(
            jax.ShapeDtypeStruct((rows_dev, d_dev), bf16),
            jax.ShapeDtypeStruct((width // n_dp, d_dev), f32),
            jax.ShapeDtypeStruct((width // n_dp, d_dev), bf16),
            jax.ShapeDtypeStruct((8, width), f32),
        ),
        in_specs=[VMEM] * 5 + [ANY] * 2,
        out_specs=[VMEM] * 4,
        scratch_shapes=[
            pltpu.VMEM((n_tensor, capacity, width), bf16),
            pltpu.VMEM((n_tensor, capacity, kv_width), bf16),
            pltpu.VMEM((NZ, rows_dev, d_dev), bf16),
            pltpu.VMEM(kv_weight.shape, bf16),
            pltpu.VMEM(connector.shape, bf16),
            pltpu.VMEM((share, width), f32),
            pltpu.VMEM((share, width), f32),
            pltpu.VMEM((share, width), bf16),
            pltpu.VMEM((NZ, 2, share, BLOCK), bf16),
            pltpu.VMEM((2, NZ, n_tensor, share, BLOCK), bf16),
            pltpu.VMEM((rows_dev, slots), bf16),
            pltpu.VMEM((rows_dev, width), bf16),
            pltpu.VMEM((rows_dev, kv_width), bf16),
            pltpu.VMEM((rows_dev, width), f32),
            pltpu.VMEM((n_dp * per_dev, rows_dev), bf16),
            pltpu.VMEM((NZ, 8, width), bf16),
            pltpu.VMEM((NZ, 8, width), bf16),
            pltpu.VMEM((BLOCK, d_dev), bf16),
            pltpu.VMEM((BLOCK, d_dev), bf16),
            pltpu.VMEM((8, width), f32),
            pltpu.VMEM((8, width), f32),
            pltpu.VMEM((BLOCK, d_dev), f32),
            pltpu.VMEM((1, width), f32),
            pltpu.SemaphoreType.DMA((keys,)),
            pltpu.SemaphoreType.DMA((keys,)),
            pltpu.SemaphoreType.DMA((6,)),
        ],
        compiler_params=pltpu.CompilerParams(
            collective_id=0, has_side_effects=True, vmem_limit_bytes=60 * 1024 * 1024
        ),
    )(
        talker_in,
        kv_grad,
        hidden,
        norm_gain.reshape(width // 128, 128),
        routing.T,
        kv_weight,
        connector,
    )
    factor = 1.0 / math.sqrt(rows_dev * n_dp)
    hidden_grad, connector_grad, weight_grad = pl.pallas_call(
        functools.partial(close, factor),
        out_shape=(
            jax.ShapeDtypeStruct((rows_dev, d_dev), bf16),
            jax.ShapeDtypeStruct((width // n_dp, d_dev), f32),
            jax.ShapeDtypeStruct((per_dev, width), f32),
        ),
        in_specs=[VMEM] * 4,
        out_specs=[VMEM] * 3,
    )(hidden_rows, own_sum, swapped, weight_sums)
    return (hidden_grad, connector_grad.T, weight_grad.T)


def solution(mesh):
    return jax.shard_map(
        on_device,
        mesh=mesh,
        in_specs=(
            P("dp", "tensor"),
            P("tensor", None),
            P("dp", None),
            P(("dp", "tensor"), None),
            P(),
            P(),
            P(("dp", "tensor"), None),
        ),
        out_specs=(P("dp", "tensor"), P("tensor", "dp"), P(None, ("dp", "tensor"))),
        check_vma=False,
    )
```

```python
import functools
import math

import jax
import jax.numpy as jnp
from jax import lax
from jax.experimental import pallas as pl
from jax.experimental.pallas import tpu as pltpu
from jax.sharding import PartitionSpec as P

MESH = pl.DeviceIdType.MESH
CONTRACT_LAST = (((1,), (1,)), ((), ()))
CONTRACT_FIRST = (((0,), (0,)), ((), ()))

NZ = 8
NY = 4


class Place:
    def __init__(self):
        self.dp = lax.axis_index("dp")
        self.t = lax.axis_index("tensor")
        self.z = lax.rem(self.dp, NZ)
        self.xl = lax.div(self.dp, NZ)
        self.core = lax.rem(self.t, 2)
        self.y = lax.rem(lax.div(self.t, 2), NY)
        self.xh = lax.div(self.t, 2 * NY)

    def tensor(self, xh, y, core):
        return xh * (2 * NY) + lax.rem(y + NY, NY) * 2 + core

    def at_y(self, step):
        return (self.dp, self.tensor(self.xh, self.y + step, self.core))

    def at_z(self, step):
        return (self.xl * NZ + lax.rem(self.z + step + NZ, NZ), self.t)

    def across(self):
        return (self.dp, self.tensor(1 - self.xh, self.y, self.core))

    def sibling(self):
        return (self.dp, self.tensor(self.xh, self.y, 1 - self.core))


def greet(devices):
    barrier = pltpu.get_barrier_semaphore()
    for device in devices:
        pl.semaphore_signal(barrier, inc=1, device_id=device, device_id_type=MESH)
    pl.semaphore_wait(barrier, len(devices))


class Sends:
    def __init__(self, send_sems, recv_sems):
        self.send_sems, self.recv_sems = send_sems, recv_sems
        self.open = []

    def send(self, src, dst, key, device):
        copy = pltpu.make_async_remote_copy(
            src_ref=src,
            dst_ref=dst,
            send_sem=self.send_sems.at[key],
            recv_sem=self.recv_sems.at[key],
            device_id=device,
            device_id_type=MESH,
        )
        copy.start()
        self.open.append(copy)

    def arrived(self, dst, key, device):
        pltpu.make_async_remote_copy(
            src_ref=dst,
            dst_ref=dst,
            send_sem=self.send_sems.at[key],
            recv_sem=self.recv_sems.at[key],
            device_id=device,
            device_id_type=MESH,
        ).wait_recv()

    def drain(self):
        for copy in self.open:
            copy.wait_send()


GROUP_KEYS = 12 + 2 + 16


def key_y(direction, far, kind):
    return direction * 6 + far * 3 + kind


def key_x(half):
    return 12 + half


def key_s(hop, half):
    return 14 + hop * 2 + half


class GroupGather:
    def __init__(self, place, own, slot, sends, base):
        self.place, self.own, self.slot = place, own, slot
        self.sends, self.base = sends, base

    def block(self, far, step):
        p = self.place
        return p.tensor(1 - p.xh if far else p.xh, p.y + step, p.core)

    def twin(self, far, step):
        p = self.place
        return p.tensor(1 - p.xh if far else p.xh, p.y + step, 1 - p.core)

    def hop(self, far, step):
        return far * 4 + step % 4

    def share(self, src, far, step, half):
        self.sends.send(
            src,
            self.slot(self.block(far, step), half),
            self.base + key_s(self.hop(far, step), half),
            self.place.sibling(),
        )

    def to_y(self, src, far, half, direction):
        step = 1 if direction == 0 else -1
        self.sends.send(
            src,
            self.slot(self.block(far, 0), half),
            self.base + key_y(direction, far, half),
            self.place.at_y(step),
        )

    def start(self, halves=(0, 1)):
        for half in halves:
            self.to_y(self.own(half), 0, half, half)
            self.to_y(self.own(half), 0, half, 1 - half)
            self.across_first(half)
        for half in halves:
            self.share(self.own(half), 0, 0, half)

    def across_first(self, half):
        self.sends.send(
            self.own(half),
            self.slot(self.block(0, 0), half),
            self.base + key_x(half),
            self.place.across(),
        )

    def take_x(self, half):
        dst = self.slot(self.block(1, 0), half)
        self.sends.arrived(dst, self.base + key_x(half), self.place.across())
        self.to_y(dst, 1, half, 0)
        self.to_y(dst, 1, half, 1)
        self.share(dst, 1, 0, half)

    def take_y(self, far, half, direction):
        step = -1 if direction == 0 else 1
        dst = self.slot(self.block(far, step), half)
        self.sends.arrived(
            dst, self.base + key_y(direction, far, half), self.place.at_y(step)
        )
        if half == direction:
            self.sends.send(
                dst,
                dst,
                self.base + key_y(direction, far, 2),
                self.place.at_y(-step),
            )
        self.share(dst, far, step, half)

    def take_far(self, far, direction):
        step = -1 if direction == 0 else 1
        half = direction
        dst = self.slot(self.block(far, 2 * step), half)
        self.sends.arrived(
            dst, self.base + key_y(direction, far, 2), self.place.at_y(step)
        )
        self.share(dst, far, 2, half)

    def take_shared(self, halves=(0, 1)):
        for far in (0, 1):
            for step in (0, 1, 2, 3):
                for half in halves:
                    self.sends.arrived(
                        self.slot(self.twin(far, step), half),
                        self.base + key_s(self.hop(far, step), half),
                        self.place.sibling(),
                    )


class GatherFromY(GroupGather):
    def across_first(self, half):
        self.to_x(self.own(half), 0, half)

    def to_x(self, src, step, half):
        self.sends.send(
            src,
            self.slot(self.block(0, step), half),
            self.base + key_from_y(step, half),
            self.place.across(),
        )

    def take_y(self, far, half, direction):
        super().take_y(0, half, direction)
        step = -1 if direction == 0 else 1
        self.to_x(self.slot(self.block(0, step), half), step, half)

    def take_far(self, far, direction):
        super().take_far(0, direction)
        self.to_x(self.slot(self.block(0, 2), direction), 2, direction)

    def take_x(self, step, half):
        dst = self.slot(self.block(1, step), half)
        self.sends.arrived(dst, self.base + key_from_y(step, half), self.place.across())
        self.share(dst, 1, step, half)


def key_from_y(step, half):
    return (3, 4, 5, 9, 10, 11, 12, 13)[(step % 4) * 2 + half]


TILE = 512
BLOCK = 256
WINDOW = 384


def onehot(rows):
    return jnp.where(rows, 1.0, 0.0).astype(jnp.bfloat16)


def dot(a, b, contract):
    return lax.dot_general(a, b, (contract, ((), ())), preferred_element_type=jnp.float32)


NN = ((1,), (0,))
NT = ((1,), (1,))
TN = ((0,), (0,))


def whole(
    talker_ref, kv_ref, hidden_ref, gain_rows_ref, route_ref, weight_any, connector_any,
    hidden_grad_ref, own_sum_ref, swapped_ref, weight_sums_ref,
    talkers, kvs, hiddens, weight, connector,
    local_rows, local_back, local_grad, packed, blocks, shifts, pick, rows, kv_rows, back, columns, terms, terms_in,
    away, away_in, sums, sums_out, sums_in, total, gain_ref, send_sems, recv_sems, own_sems,
):
    bf16, f32 = jnp.bfloat16, jnp.float32
    place = Place()
    width = talker_ref.shape[1]
    tiles = width // TILE
    capacity = talker_ref.shape[0]
    n_tensor = talkers.shape[0]
    slots = n_tensor * capacity
    rows_dev = hidden_ref.shape[0]
    share = rows_dev // n_tensor
    piece_rows = own_sum_ref.shape[0]
    loads = [
        pltpu.make_async_copy(weight_any, weight, own_sems.at[0]),
        pltpu.make_async_copy(connector_any, connector, own_sems.at[1]),
    ]
    for load in loads:
        load.start()
    over_x = (lax.rem(place.dp + NZ, 2 * NZ), place.t)
    greet(
        [place.at_z(step) for step in range(1, NZ)]
        + [place.at_y(1), place.at_y(-1), place.across(), place.sibling(), over_x]
    )
    sends = Sends(send_sems, recv_sems)
    half_rows = capacity // 2
    half_hidden = rows_dev // 2
    kept = [
        pltpu.make_async_copy(talker_ref, talkers.at[place.t], own_sems.at[2]),
        pltpu.make_async_copy(kv_ref, kvs.at[place.t], own_sems.at[3]),
        pltpu.make_async_copy(hidden_ref, hiddens.at[place.z], own_sems.at[4]),
    ]

    def tile_of(i):
        return pl.ds(pl.multiple_of(i * TILE, TILE), TILE)

    def gather(kind, own_ref, where, base):
        return kind(
            place,
            lambda half: own_ref.at[pl.ds(half * half_rows, half_rows)],
            lambda block, half: where.at[block, pl.ds(half * half_rows, half_rows)],
            sends,
            base,
        )

    wide = gather(GroupGather, talker_ref, talkers, 0)
    thin = gather(GatherFromY, kv_ref, kvs, GROUP_KEYS)

    def block_slot(block, half):
        return blocks.at[lax.rem(1 - place.xl + half, 2), :, block]

    def own_block(half):
        return block_slot(place.t, half)

    theirs = GroupGather(place, own_block, block_slot, sends, 2 * GROUP_KEYS)
    ours = GatherFromY(place, own_block, block_slot, sends, 3 * GROUP_KEYS)
    z_base = 4 * GROUP_KEYS
    packed_base = z_base + NZ
    terms_base = packed_base + NZ
    x_base = terms_base + NZ

    def z_at(step):
        return lax.rem(place.z + step + NZ, NZ)

    def z_slot(step, part=None):
        slot = hiddens.at[z_at(step)]
        if part is None:
            return slot
        return slot.at[pl.ds(part * half_hidden, half_hidden)]

    def pass_z(hop):
        for direction, step in ((0, -1), (1, 1)):
            if hop:
                sends.arrived(z_slot(hop * step), z_base + direction * 4 + hop - 1, place.at_z(step))
            part = direction if hop == 3 else None
            src = z_slot(hop * step, part) if hop else hidden_ref
            sends.send(
                src, z_slot(hop * step, part), z_base + direction * 4 + hop, place.at_z(-step)
            )

    def to_all_z(src, dst, base):
        for step in (1, 7, 2, 6, 3, 5, 4):
            sends.send(src(step), dst, base + step, place.at_z(step))

    def from_all_z(dst, base):
        for step in (1, 7, 2, 6, 3, 5, 4):
            sends.arrived(dst(-step), base + step, place.at_z(-step))

    def number_rows():
        route = route_ref[...]
        shard = lax.broadcasted_iota(jnp.int32, (n_tensor, rows_dev), 0)
        named = shard == route
        earlier = lax.broadcasted_iota(jnp.int32, (rows_dev, rows_dev), 0)
        later = lax.broadcasted_iota(jnp.int32, (rows_dev, rows_dev), 1)
        before = dot(onehot(named), onehot(earlier < later), NN)
        rank = jnp.sum(jnp.where(named, before, 0.0), axis=0, keepdims=True)
        slot = route * capacity + rank.astype(jnp.int32)
        slot_at = lax.broadcasted_iota(jnp.int32, (slots, rows_dev), 0)
        same = onehot(earlier == later)
        pick[...] = dot(same, onehot(slot_at == slot), NT).astype(bf16)
        lanes = gain_rows_ref.shape[1]
        for i in range(gain_rows_ref.shape[0]):
            gain_ref[:, i * lanes : (i + 1) * lanes] = gain_rows_ref[i : i + 1, :]

    def own_rows():
        mine = pl.ds(pl.multiple_of(place.t * share, share), share)
        kv_all = kvs[...].reshape(slots, kvs.shape[2])
        kv_rows[...] = dot(pick[...], kv_all, NN).astype(bf16)

        def first(i, carry):
            squares, products = carry
            tile = tile_of(i)
            inputs = dot(pick[mine, :], talkers[:, :, tile].reshape(slots, TILE), NN)
            local_rows[:, tile] = inputs
            gained = gain_ref[:, tile] * dot(kv_rows[mine, :], weight[tile, :], NT)
            local_back[:, tile] = gained
            return (
                squares + jnp.sum(inputs * inputs, axis=1, keepdims=True),
                products + jnp.sum(gained * inputs, axis=1, keepdims=True),
            )

        zero = jnp.zeros((share, 1), f32)
        squares, products = lax.fori_loop(0, tiles, first, (zero, zero))
        inv_rms = lax.rsqrt(squares / width + 1e-06)
        mean = products * inv_rms / width

        def second(i, carry):
            tile = tile_of(i)
            scaled = local_rows[:, tile] * inv_rms
            local_grad[:, tile] = (inv_rms * (local_back[:, tile] - scaled * mean)).astype(bf16)
            return carry

        lax.fori_loop(0, tiles, second, 0)
        for index in range(2 * NZ):
            start, kind = cuts[index]
            packed[index % NZ, index // NZ] = dot(
                local_grad[:, start : start + WINDOW], shifts[kind], NN
            ).astype(bf16)

    def make_shifts():
        window_at = lax.broadcasted_iota(jnp.int32, (WINDOW, BLOCK), 0)
        wanted = lax.broadcasted_iota(jnp.int32, (WINDOW, BLOCK), 1)
        for kind, offset in enumerate(offsets):
            shifts[kind] = onehot((window_at == wanted + offset) & (wanted < piece))

    def pick_rows():
        at = lax.broadcasted_iota(jnp.int32, columns_shape, 0)
        col = lax.broadcasted_iota(jnp.int32, columns_shape, 1)
        dp = ((at >> 2) & 1) * NZ + (at >> 3)
        chosen = onehot(col == (dp * n_tensor + place.t) * 4 + (at & 3))
        columns[...] = dot(chosen, kv_rows[...], NT).astype(bf16)

        def one(i, squares):
            tile = tile_of(i)
            inputs = dot(pick[...], talkers[:, :, tile].reshape(slots, TILE), NN)
            rows[:, tile] = inputs.astype(bf16)
            return squares + jnp.sum(inputs * inputs, axis=1, keepdims=True)

        squares = lax.fori_loop(0, tiles, one, jnp.zeros((rows_dev, 1), f32))
        return lax.rsqrt(squares / width + 1e-06)

    piece = width // (2 * NZ)
    starts = [min(i * piece // 128 * 128, width - WINDOW) for i in range(2 * NZ)]
    offsets = sorted({i * piece - start for i, start in enumerate(starts)})
    cuts = [(start, offsets.index(i * piece - start)) for i, start in enumerate(starts)]
    columns_shape = (terms.shape[0] * terms.shape[1], kv_ref.shape[1])

    def make_terms(inv_rms):
        def one(i, carry):
            tile = tile_of(i)
            normed = ((rows[:, tile].astype(f32) * inv_rms) * gain_ref[:, tile]).astype(bf16)
            term = dot(columns[...], normed, NN)
            for at in range(NZ):
                terms[at, :, tile] = term[at * 8 : (at + 1) * 8].astype(bf16)
            return carry

        lax.fori_loop(0, tiles, one, 0)

    def make_back(first, last, products):
        def one(i, products):
            tile = tile_of(i)
            gained = gain_ref[:, tile] * dot(kv_rows[...], weight[tile, :], NT)
            back[:, tile] = gained
            return products + jnp.sum(gained * rows[:, tile].astype(f32), axis=1, keepdims=True)

        return lax.fori_loop(first, last, one, products)

    def make_hidden_grad(inv_rms, products):
        mean = products * inv_rms / width
        total[...] = jnp.zeros_like(total)

        def one(i, carry):
            tile = tile_of(i)
            scaled = rows[:, tile].astype(f32) * inv_rms
            grad = (inv_rms * (back[:, tile] - scaled * mean)).astype(bf16)
            total[...] += dot(grad, connector[:, tile], NT)
            return carry

        lax.fori_loop(0, tiles, one, 0)
        hidden_grad_ref[...] = total[...].astype(bf16)

    def connector_part(block):
        part = NZ // 4
        total[...] = jnp.zeros_like(total)

        def one(i, carry):
            at = pl.ds(i * part, part)
            lhs = blocks[block, at].reshape(part * rows_dev, BLOCK)
            rhs = hiddens[at].reshape(part * rows_dev, hiddens.shape[2])
            total[...] += dot(lhs, rhs, TN)
            return carry

        lax.fori_loop(0, 4, one, 0)

    wide.start()
    thin.start()
    pass_z(0)
    for copy in kept:
        copy.start()
    number_rows()
    make_shifts()
    for direction in (0, 1):
        wide.take_y(0, direction, direction)
    wide.take_x(0)
    for direction in (0, 1):
        wide.take_y(0, 1 - direction, direction)
    wide.take_x(1)
    pass_z(1)
    for half in (0, 1):
        for direction in (half, 1 - half):
            thin.take_y(0, half, direction)
    for direction in (0, 1):
        wide.take_far(0, direction)
        thin.take_far(0, direction)
    for direction in (0, 1):
        wide.take_y(1, direction, direction)
    pass_z(2)
    for direction in (0, 1):
        wide.take_y(1, 1 - direction, direction)
    for step in (0, 1, -1, 2):
        for half in (0, 1):
            thin.take_x(step, half)
    for direction in (0, 1):
        wide.take_far(1, direction)
    thin.take_shared()
    wide.take_shared()
    kept[0].wait()
    kept[1].wait()
    loads[0].wait()
    own_rows()
    own_packed = pltpu.make_async_copy(
        packed.at[place.z], blocks.at[:, place.z, place.t], own_sems.at[5]
    )
    own_packed.start()
    to_all_z(lambda step: packed.at[z_at(step)], blocks.at[:, place.z, place.t], packed_base)
    pass_z(3)
    inv_rms = pick_rows()
    make_terms(inv_rms)
    from_all_z(lambda step: blocks.at[:, z_at(step), place.t], packed_base)
    own_packed.wait()
    theirs.start((0,))
    ours.start((1,))
    to_all_z(lambda step: terms.at[z_at(step)], terms_in.at[place.z], terms_base)
    products = make_back(0, tiles, jnp.zeros((rows_dev, 1), f32))
    ours.take_y(0, 1, 1)
    theirs.take_y(0, 0, 0)
    ours.take_y(0, 1, 0)
    theirs.take_y(0, 0, 1)
    theirs.take_x(0)
    ours.take_far(0, 1)
    ours.take_x(0, 1)
    theirs.take_far(0, 0)
    theirs.take_y(1, 0, 0)
    theirs.take_y(1, 0, 1)
    for step in (1, -1):
        ours.take_x(step, 1)
    theirs.take_far(1, 0)
    ours.take_x(2, 1)
    for direction, step in ((0, -1), (1, 1)):
        sends.arrived(z_slot(4 * step, direction), z_base + direction * 4 + 3, place.at_z(step))
    kept[2].wait()
    theirs.take_shared((0,))
    connector_part(1 - place.xl)
    away[...] = total[...].astype(bf16)
    sends.send(
        away.at[pl.ds(0, piece_rows)], away_in.at[pl.ds(0, piece_rows)], x_base, over_x
    )
    from_all_z(lambda step: terms_in.at[z_at(step)], terms_base)
    terms_in[place.z] = terms[place.z]

    def add_up(i, carry):
        tile = tile_of(i)
        added = jnp.sum(terms_in[:, :, tile].astype(f32), axis=0)
        sums[:, tile] = added
        sums_out[:, tile] = added.astype(bf16)
        return carry

    lax.fori_loop(0, tiles, add_up, 0)
    sends.send(sums_out, sums_in, x_base + 1, over_x)
    loads[1].wait()
    make_hidden_grad(inv_rms, products)
    ours.take_shared((1,))
    connector_part(place.xl)
    own_sum_ref[...] = total[0:piece_rows, :]
    sends.arrived(sums_in, x_base + 1, over_x)
    weight_sums_ref[...] = sums[...] + sums_in[...].astype(f32)
    sends.arrived(away_in.at[pl.ds(0, piece_rows)], x_base, over_x)
    swapped_ref[...] = away_in[0:piece_rows, :]
    sends.drain()


def close(factor, hidden_ref, own_ref, swapped_ref, sums_ref, hidden_grad_ref, connector_grad_ref, weight_grad_ref):
    hidden_grad_ref[...] = hidden_ref[...]
    connector_grad_ref[...] = (own_ref[...] + swapped_ref[...].astype(jnp.float32)) * factor
    sums = sums_ref[...]
    mine = jnp.where(lax.axis_index("dp") < NZ, sums[0:4], sums[4:8])
    weight_grad_ref[...] = mine * factor


VMEM = pl.BlockSpec(memory_space=pltpu.VMEM)
ANY = pl.BlockSpec(memory_space=pl.ANY)


def on_device(hidden, connector, routing, talker_in, norm_gain, kv_weight, kv_grad):
    n_dp = lax.axis_size("dp")
    n_tensor = lax.axis_size("tensor")
    rows_dev, d_dev = hidden.shape
    capacity, width = talker_in.shape
    kv_width = kv_grad.shape[1]
    slots = n_tensor * capacity
    share = rows_dev // n_tensor
    per_dev = kv_width // (n_dp * n_tensor)
    bf16, f32 = jnp.bfloat16, jnp.float32

    keys = 4 * GROUP_KEYS + 3 * NZ + 2
    hidden_rows, own_sum, swapped, weight_sums = pl.pallas_call(
        whole,
        out_shape=(
            jax.ShapeDtypeStruct((rows_dev, d_dev), bf16),
            jax.ShapeDtypeStruct((width // n_dp, d_dev), f32),
            jax.ShapeDtypeStruct((width // n_dp, d_dev), bf16),
            jax.ShapeDtypeStruct((8, width), f32),
        ),
        in_specs=[VMEM] * 5 + [ANY] * 2,
        out_specs=[VMEM] * 4,
        scratch_shapes=[
            pltpu.VMEM((n_tensor, capacity, width), bf16),
            pltpu.VMEM((n_tensor, capacity, kv_width), bf16),
            pltpu.VMEM((NZ, rows_dev, d_dev), bf16),
            pltpu.VMEM(kv_weight.shape, bf16),
            pltpu.VMEM(connector.shape, bf16),
            pltpu.VMEM((share, width), f32),
            pltpu.VMEM((share, width), f32),
            pltpu.VMEM((share, width), bf16),
            pltpu.VMEM((NZ, 2, share, BLOCK), bf16),
            pltpu.VMEM((2, NZ, n_tensor, share, BLOCK), bf16),
            pltpu.VMEM((8, WINDOW, BLOCK), bf16),
            pltpu.VMEM((rows_dev, slots), bf16),
            pltpu.VMEM((rows_dev, width), bf16),
            pltpu.VMEM((rows_dev, kv_width), bf16),
            pltpu.VMEM((rows_dev, width), f32),
            pltpu.VMEM((n_dp * per_dev, rows_dev), bf16),
            pltpu.VMEM((NZ, 8, width), bf16),
            pltpu.VMEM((NZ, 8, width), bf16),
            pltpu.VMEM((BLOCK, d_dev), bf16),
            pltpu.VMEM((BLOCK, d_dev), bf16),
            pltpu.VMEM((8, width), f32),
            pltpu.VMEM((8, width), bf16),
            pltpu.VMEM((8, width), bf16),
            pltpu.VMEM((BLOCK, d_dev), f32),
            pltpu.VMEM((1, width), f32),
            pltpu.SemaphoreType.DMA((keys,)),
            pltpu.SemaphoreType.DMA((keys,)),
            pltpu.SemaphoreType.DMA((6,)),
        ],
        compiler_params=pltpu.CompilerParams(
            collective_id=0, has_side_effects=True, vmem_limit_bytes=60 * 1024 * 1024
        ),
    )(
        talker_in,
        kv_grad,
        hidden,
        norm_gain.reshape(width // 128, 128),
        routing.T,
        kv_weight,
        connector,
    )
    factor = 1.0 / math.sqrt(rows_dev * n_dp)
    hidden_grad, connector_grad, weight_grad = pl.pallas_call(
        functools.partial(close, factor),
        out_shape=(
            jax.ShapeDtypeStruct((rows_dev, d_dev), bf16),
            jax.ShapeDtypeStruct((width // n_dp, d_dev), f32),
            jax.ShapeDtypeStruct((per_dev, width), f32),
        ),
        in_specs=[VMEM] * 4,
        out_specs=[VMEM] * 3,
    )(hidden_rows, own_sum, swapped, weight_sums)
    return (hidden_grad, connector_grad.T, weight_grad.T)


def solution(mesh):
    return jax.shard_map(
        on_device,
        mesh=mesh,
        in_specs=(
            P("dp", "tensor"),
            P("tensor", None),
            P("dp", None),
            P(("dp", "tensor"), None),
            P(),
            P(),
            P(("dp", "tensor"), None),
        ),
        out_specs=(P("dp", "tensor"), P("tensor", "dp"), P(None, ("dp", "tensor"))),
        check_vma=False,
    )
```

```python
import functools
import math

import jax
import jax.numpy as jnp
from jax import lax
from jax.experimental import pallas as pl
from jax.experimental.pallas import tpu as pltpu
from jax.sharding import PartitionSpec as P

MESH = pl.DeviceIdType.MESH
CONTRACT_LAST = (((1,), (1,)), ((), ()))
CONTRACT_FIRST = (((0,), (0,)), ((), ()))

NZ = 8
NY = 4


class Place:
    def __init__(self):
        self.dp = lax.axis_index("dp")
        self.t = lax.axis_index("tensor")
        self.z = lax.rem(self.dp, NZ)
        self.xl = lax.div(self.dp, NZ)
        self.core = lax.rem(self.t, 2)
        self.y = lax.rem(lax.div(self.t, 2), NY)
        self.xh = lax.div(self.t, 2 * NY)

    def tensor(self, xh, y, core):
        return xh * (2 * NY) + lax.rem(y + NY, NY) * 2 + core

    def at_y(self, step):
        return (self.dp, self.tensor(self.xh, self.y + step, self.core))

    def at_z(self, step):
        return (self.xl * NZ + lax.rem(self.z + step + NZ, NZ), self.t)

    def across(self):
        return (self.dp, self.tensor(1 - self.xh, self.y, self.core))

    def sibling(self):
        return (self.dp, self.tensor(self.xh, self.y, 1 - self.core))


def greet(devices):
    barrier = pltpu.get_barrier_semaphore()
    for device in devices:
        pl.semaphore_signal(barrier, inc=1, device_id=device, device_id_type=MESH)
    pl.semaphore_wait(barrier, len(devices))


class Sends:
    def __init__(self, send_sems, recv_sems):
        self.send_sems, self.recv_sems = send_sems, recv_sems
        self.open = []

    def send(self, src, dst, key, device):
        copy = pltpu.make_async_remote_copy(
            src_ref=src,
            dst_ref=dst,
            send_sem=self.send_sems.at[key],
            recv_sem=self.recv_sems.at[key],
            device_id=device,
            device_id_type=MESH,
        )
        copy.start()
        self.open.append(copy)

    def arrived(self, dst, key, device):
        pltpu.make_async_remote_copy(
            src_ref=dst,
            dst_ref=dst,
            send_sem=self.send_sems.at[key],
            recv_sem=self.recv_sems.at[key],
            device_id=device,
            device_id_type=MESH,
        ).wait_recv()

    def drain(self):
        for copy in self.open:
            copy.wait_send()


GROUP_KEYS = 12 + 2 + 16


def key_y(direction, far, kind):
    return direction * 6 + far * 3 + kind


def key_x(half):
    return 12 + half


def key_s(hop, half):
    return 14 + hop * 2 + half


class GroupGather:
    def __init__(self, place, own, slot, sends, base):
        self.place, self.own, self.slot = place, own, slot
        self.sends, self.base = sends, base

    def block(self, far, step):
        p = self.place
        return p.tensor(1 - p.xh if far else p.xh, p.y + step, p.core)

    def twin(self, far, step):
        p = self.place
        return p.tensor(1 - p.xh if far else p.xh, p.y + step, 1 - p.core)

    def hop(self, far, step):
        return far * 4 + step % 4

    def share(self, src, far, step, half):
        self.sends.send(
            src,
            self.slot(self.block(far, step), half),
            self.base + key_s(self.hop(far, step), half),
            self.place.sibling(),
        )

    def to_y(self, src, far, half, direction):
        step = 1 if direction == 0 else -1
        self.sends.send(
            src,
            self.slot(self.block(far, 0), half),
            self.base + key_y(direction, far, half),
            self.place.at_y(step),
        )

    def start(self, halves=(0, 1)):
        for half in halves:
            self.to_y(self.own(half), 0, half, half)
            self.to_y(self.own(half), 0, half, 1 - half)
            self.across_first(half)
        for half in halves:
            self.share(self.own(half), 0, 0, half)

    def across_first(self, half):
        self.sends.send(
            self.own(half),
            self.slot(self.block(0, 0), half),
            self.base + key_x(half),
            self.place.across(),
        )

    def take_x(self, half):
        dst = self.slot(self.block(1, 0), half)
        self.sends.arrived(dst, self.base + key_x(half), self.place.across())
        self.to_y(dst, 1, half, 0)
        self.to_y(dst, 1, half, 1)
        self.share(dst, 1, 0, half)

    def take_y(self, far, half, direction):
        step = -1 if direction == 0 else 1
        dst = self.slot(self.block(far, step), half)
        self.sends.arrived(
            dst, self.base + key_y(direction, far, half), self.place.at_y(step)
        )
        if half == direction:
            self.sends.send(
                dst,
                dst,
                self.base + key_y(direction, far, 2),
                self.place.at_y(-step),
            )
        self.share(dst, far, step, half)

    def take_far(self, far, direction):
        step = -1 if direction == 0 else 1
        half = direction
        dst = self.slot(self.block(far, 2 * step), half)
        self.sends.arrived(
            dst, self.base + key_y(direction, far, 2), self.place.at_y(step)
        )
        self.share(dst, far, 2, half)

    def take_shared(self, halves=(0, 1)):
        for far in (0, 1):
            for step in (0, 1, 2, 3):
                for half in halves:
                    self.sends.arrived(
                        self.slot(self.twin(far, step), half),
                        self.base + key_s(self.hop(far, step), half),
                        self.place.sibling(),
                    )


class GatherFromY(GroupGather):
    def across_first(self, half):
        self.to_x(self.own(half), 0, half)

    def to_x(self, src, step, half):
        self.sends.send(
            src,
            self.slot(self.block(0, step), half),
            self.base + key_from_y(step, half),
            self.place.across(),
        )

    def take_y(self, far, half, direction):
        super().take_y(0, half, direction)
        step = -1 if direction == 0 else 1
        self.to_x(self.slot(self.block(0, step), half), step, half)

    def take_far(self, far, direction):
        super().take_far(0, direction)
        self.to_x(self.slot(self.block(0, 2), direction), 2, direction)

    def take_x(self, step, half):
        dst = self.slot(self.block(1, step), half)
        self.sends.arrived(dst, self.base + key_from_y(step, half), self.place.across())
        self.share(dst, 1, step, half)


def key_from_y(step, half):
    return (3, 4, 5, 9, 10, 11, 12, 13)[(step % 4) * 2 + half]


TILE = 512
BLOCK = 256
WINDOW = 384


def onehot(rows):
    return jnp.where(rows, 1.0, 0.0).astype(jnp.bfloat16)


def dot(a, b, contract):
    return lax.dot_general(a, b, (contract, ((), ())), preferred_element_type=jnp.float32)


NN = ((1,), (0,))
NT = ((1,), (1,))
TN = ((0,), (0,))


def whole(
    talker_ref, kv_ref, hidden_ref, gain_rows_ref, route_ref, weight_any, connector_any,
    hidden_grad_ref, own_sum_ref, swapped_ref, weight_sums_ref,
    talkers, kvs, hiddens, weight, connector,
    local_rows, local_grad, packed, blocks, shifts, pick, rows, kv_rows, back, columns, terms, terms_in,
    away, away_in, sums, sums_out, sums_in, total, gain_ref, send_sems, recv_sems, own_sems,
):
    bf16, f32 = jnp.bfloat16, jnp.float32
    place = Place()
    width = talker_ref.shape[1]
    tiles = width // TILE
    capacity = talker_ref.shape[0]
    n_tensor = talkers.shape[0]
    slots = n_tensor * capacity
    rows_dev = hidden_ref.shape[0]
    share = rows_dev // n_tensor
    piece_rows = own_sum_ref.shape[0]
    loads = [
        pltpu.make_async_copy(weight_any, weight, own_sems.at[0]),
        pltpu.make_async_copy(connector_any, connector, own_sems.at[1]),
    ]
    for load in loads:
        load.start()
    over_x = (lax.rem(place.dp + NZ, 2 * NZ), place.t)
    greet(
        [place.at_z(step) for step in range(1, NZ)]
        + [place.at_y(1), place.at_y(-1), place.across(), place.sibling(), over_x]
    )
    sends = Sends(send_sems, recv_sems)
    half_rows = capacity // 2
    half_hidden = rows_dev // 2
    kept = [
        pltpu.make_async_copy(talker_ref, talkers.at[place.t], own_sems.at[2]),
        pltpu.make_async_copy(kv_ref, kvs.at[place.t], own_sems.at[3]),
        pltpu.make_async_copy(hidden_ref, hiddens.at[place.z], own_sems.at[4]),
    ]

    def tile_of(i):
        return pl.ds(pl.multiple_of(i * TILE, TILE), TILE)

    def gather(kind, own_ref, where, base):
        return kind(
            place,
            lambda half: own_ref.at[pl.ds(half * half_rows, half_rows)],
            lambda block, half: where.at[block, pl.ds(half * half_rows, half_rows)],
            sends,
            base,
        )

    wide = gather(GroupGather, talker_ref, talkers, 0)
    thin = gather(GatherFromY, kv_ref, kvs, GROUP_KEYS)

    def block_slot(block, half):
        return blocks.at[lax.rem(1 - place.xl + half, 2), :, block]

    def own_block(half):
        return block_slot(place.t, half)

    theirs = GroupGather(place, own_block, block_slot, sends, 2 * GROUP_KEYS)
    ours = GatherFromY(place, own_block, block_slot, sends, 3 * GROUP_KEYS)
    z_base = 4 * GROUP_KEYS
    packed_base = z_base + NZ
    terms_base = packed_base + NZ
    x_base = terms_base + NZ

    def z_at(step):
        return lax.rem(place.z + step + NZ, NZ)

    def z_slot(step, part=None):
        slot = hiddens.at[z_at(step)]
        if part is None:
            return slot
        return slot.at[pl.ds(part * half_hidden, half_hidden)]

    def pass_z(hop):
        for direction, step in ((0, -1), (1, 1)):
            if hop:
                sends.arrived(z_slot(hop * step), z_base + direction * 4 + hop - 1, place.at_z(step))
            part = direction if hop == 3 else None
            src = z_slot(hop * step, part) if hop else hidden_ref
            sends.send(
                src, z_slot(hop * step, part), z_base + direction * 4 + hop, place.at_z(-step)
            )

    def to_all_z(src, dst, base):
        for step in (1, 7, 2, 6, 3, 5, 4):
            sends.send(src(step), dst, base + step, place.at_z(step))

    def from_all_z(dst, base):
        for step in (1, 7, 2, 6, 3, 5, 4):
            sends.arrived(dst(-step), base + step, place.at_z(-step))

    def number_rows():
        route = route_ref[...]
        shard = lax.broadcasted_iota(jnp.int32, (n_tensor, rows_dev), 0)
        named = shard == route
        earlier = lax.broadcasted_iota(jnp.int32, (rows_dev, rows_dev), 0)
        later = lax.broadcasted_iota(jnp.int32, (rows_dev, rows_dev), 1)
        before = dot(onehot(named), onehot(earlier < later), NN)
        rank = jnp.sum(jnp.where(named, before, 0.0), axis=0, keepdims=True)
        slot = route * capacity + rank.astype(jnp.int32)
        slot_at = lax.broadcasted_iota(jnp.int32, (slots, rows_dev), 0)
        same = onehot(earlier == later)
        pick[...] = dot(same, onehot(slot_at == slot), NT).astype(bf16)
        lanes = gain_rows_ref.shape[1]
        for i in range(gain_rows_ref.shape[0]):
            gain_ref[:, i * lanes : (i + 1) * lanes] = gain_rows_ref[i : i + 1, :]

    def own_rows():
        mine = pl.ds(pl.multiple_of(place.t * share, share), share)

        def first(i, carry):
            squares, products = carry
            tile = tile_of(i)
            inputs = dot(pick[mine, :], talkers[:, :, tile].reshape(slots, TILE), NN)
            local_rows[:, tile] = inputs
            gained = back[mine, tile]
            return (
                squares + jnp.sum(inputs * inputs, axis=1, keepdims=True),
                products + jnp.sum(gained * inputs, axis=1, keepdims=True),
            )

        zero = jnp.zeros((share, 1), f32)
        squares, products = lax.fori_loop(0, tiles, first, (zero, zero))
        inv_rms = lax.rsqrt(squares / width + 1e-06)
        mean = products * inv_rms / width

        def second(i, carry):
            tile = tile_of(i)
            scaled = local_rows[:, tile] * inv_rms
            local_grad[:, tile] = (inv_rms * (back[mine, tile] - scaled * mean)).astype(bf16)
            return carry

        lax.fori_loop(0, tiles, second, 0)
        for index in range(2 * NZ):
            start, kind = cuts[index]
            packed[index % NZ, index // NZ] = dot(
                local_grad[:, start : start + WINDOW], shifts[kind], NN
            ).astype(bf16)

    def make_shifts():
        window_at = lax.broadcasted_iota(jnp.int32, (WINDOW, BLOCK), 0)
        wanted = lax.broadcasted_iota(jnp.int32, (WINDOW, BLOCK), 1)
        for kind, offset in enumerate(offsets):
            shifts[kind] = onehot((window_at == wanted + offset) & (wanted < piece))

    def pick_kv():
        kv_all = kvs[...].reshape(slots, kvs.shape[2])
        kv_rows[...] = dot(pick[...], kv_all, NN).astype(bf16)
        at = lax.broadcasted_iota(jnp.int32, columns_shape, 0)
        col = lax.broadcasted_iota(jnp.int32, columns_shape, 1)
        dp = ((at >> 2) & 1) * NZ + (at >> 3)
        chosen = onehot(col == (dp * n_tensor + place.t) * 4 + (at & 3))
        columns[...] = dot(chosen, kv_rows[...], NT).astype(bf16)

    def make_back(first, last):
        def one(i, carry):
            tile = tile_of(i)
            back[:, tile] = gain_ref[:, tile] * dot(kv_rows[...], weight[tile, :], NT)
            return carry

        lax.fori_loop(first, last, one, 0)

    def pick_rows():
        def one(i, carry):
            squares, products = carry
            tile = tile_of(i)
            inputs = dot(pick[...], talkers[:, :, tile].reshape(slots, TILE), NN)
            rows[:, tile] = inputs.astype(bf16)
            return (
                squares + jnp.sum(inputs * inputs, axis=1, keepdims=True),
                products + jnp.sum(back[:, tile] * inputs, axis=1, keepdims=True),
            )

        zero = jnp.zeros((rows_dev, 1), f32)
        squares, products = lax.fori_loop(0, tiles, one, (zero, zero))
        return lax.rsqrt(squares / width + 1e-06), products

    piece = width // (2 * NZ)
    starts = [min(i * piece // 128 * 128, width - WINDOW) for i in range(2 * NZ)]
    offsets = sorted({i * piece - start for i, start in enumerate(starts)})
    cuts = [(start, offsets.index(i * piece - start)) for i, start in enumerate(starts)]
    columns_shape = (terms.shape[0] * terms.shape[1], kv_ref.shape[1])

    def make_terms(inv_rms):
        def one(i, carry):
            tile = tile_of(i)
            normed = ((rows[:, tile].astype(f32) * inv_rms) * gain_ref[:, tile]).astype(bf16)
            term = dot(columns[...], normed, NN)
            for at in range(NZ):
                terms[at, :, tile] = term[at * 8 : (at + 1) * 8].astype(bf16)
            return carry

        lax.fori_loop(0, tiles, one, 0)

    def make_hidden_grad(inv_rms, products):
        mean = products * inv_rms / width
        total[...] = jnp.zeros_like(total)

        def one(i, carry):
            tile = tile_of(i)
            scaled = rows[:, tile].astype(f32) * inv_rms
            grad = (inv_rms * (back[:, tile] - scaled * mean)).astype(bf16)
            total[...] += dot(grad, connector[:, tile], NT)
            return carry

        lax.fori_loop(0, tiles, one, 0)
        hidden_grad_ref[...] = total[...].astype(bf16)

    def connector_part(block):
        part = NZ // 4
        total[...] = jnp.zeros_like(total)

        def one(i, carry):
            at = pl.ds(i * part, part)
            lhs = blocks[block, at].reshape(part * rows_dev, BLOCK)
            rhs = hiddens[at].reshape(part * rows_dev, hiddens.shape[2])
            total[...] += dot(lhs, rhs, TN)
            return carry

        lax.fori_loop(0, 4, one, 0)

    wide.start()
    thin.start()
    pass_z(0)
    for copy in kept:
        copy.start()
    number_rows()
    make_shifts()
    for direction in (0, 1):
        wide.take_y(0, direction, direction)
    wide.take_x(0)
    for direction in (0, 1):
        wide.take_y(0, 1 - direction, direction)
    wide.take_x(1)
    pass_z(1)
    for half in (0, 1):
        for direction in (half, 1 - half):
            thin.take_y(0, half, direction)
    for direction in (0, 1):
        wide.take_far(0, direction)
        thin.take_far(0, direction)
    for step in (0, 1, -1):
        for half in (0, 1):
            thin.take_x(step, half)
    for direction in (0, 1):
        wide.take_y(1, direction, direction)
    for half in (0, 1):
        thin.take_x(2, half)
    thin.take_shared()
    kept[1].wait()
    pick_kv()
    loads[0].wait()
    make_back(0, 3)
    for direction in (0, 1):
        wide.take_y(1, 1 - direction, direction)
    pass_z(2)
    make_back(3, tiles)
    for direction in (0, 1):
        wide.take_far(1, direction)
    wide.take_shared()
    kept[0].wait()
    own_rows()
    own_packed = pltpu.make_async_copy(
        packed.at[place.z], blocks.at[:, place.z, place.t], own_sems.at[5]
    )
    own_packed.start()
    to_all_z(lambda step: packed.at[z_at(step)], blocks.at[:, place.z, place.t], packed_base)
    pass_z(3)
    inv_rms, products = pick_rows()
    make_terms(inv_rms)
    from_all_z(lambda step: blocks.at[:, z_at(step), place.t], packed_base)
    own_packed.wait()
    theirs.start((0,))
    ours.start((1,))
    to_all_z(lambda step: terms.at[z_at(step)], terms_in.at[place.z], terms_base)
    ours.take_y(0, 1, 1)
    theirs.take_y(0, 0, 0)
    ours.take_y(0, 1, 0)
    theirs.take_y(0, 0, 1)
    theirs.take_x(0)
    ours.take_far(0, 1)
    ours.take_x(0, 1)
    theirs.take_far(0, 0)
    theirs.take_y(1, 0, 0)
    theirs.take_y(1, 0, 1)
    for step in (1, -1):
        ours.take_x(step, 1)
    theirs.take_far(1, 0)
    ours.take_x(2, 1)
    for direction, step in ((0, -1), (1, 1)):
        sends.arrived(z_slot(4 * step, direction), z_base + direction * 4 + 3, place.at_z(step))
    kept[2].wait()
    theirs.take_shared((0,))
    connector_part(1 - place.xl)
    away[...] = total[...].astype(bf16)
    sends.send(
        away.at[pl.ds(0, piece_rows)], away_in.at[pl.ds(0, piece_rows)], x_base, over_x
    )
    from_all_z(lambda step: terms_in.at[z_at(step)], terms_base)
    terms_in[place.z] = terms[place.z]

    def add_up(i, carry):
        tile = tile_of(i)
        added = jnp.sum(terms_in[:, :, tile].astype(f32), axis=0)
        sums[:, tile] = added
        sums_out[:, tile] = added.astype(bf16)
        return carry

    lax.fori_loop(0, tiles, add_up, 0)
    sends.send(sums_out, sums_in, x_base + 1, over_x)
    loads[1].wait()
    make_hidden_grad(inv_rms, products)
    ours.take_shared((1,))
    connector_part(place.xl)
    own_sum_ref[...] = total[0:piece_rows, :]
    sends.arrived(sums_in, x_base + 1, over_x)
    weight_sums_ref[...] = sums[...] + sums_in[...].astype(f32)
    sends.arrived(away_in.at[pl.ds(0, piece_rows)], x_base, over_x)
    swapped_ref[...] = away_in[0:piece_rows, :]
    sends.drain()


def close(factor, hidden_ref, own_ref, swapped_ref, sums_ref, hidden_grad_ref, connector_grad_ref, weight_grad_ref):
    hidden_grad_ref[...] = hidden_ref[...]
    connector_grad_ref[...] = (own_ref[...] + swapped_ref[...].astype(jnp.float32)) * factor
    sums = sums_ref[...]
    mine = jnp.where(lax.axis_index("dp") < NZ, sums[0:4], sums[4:8])
    weight_grad_ref[...] = mine * factor


VMEM = pl.BlockSpec(memory_space=pltpu.VMEM)
ANY = pl.BlockSpec(memory_space=pl.ANY)


def on_device(hidden, connector, routing, talker_in, norm_gain, kv_weight, kv_grad):
    n_dp = lax.axis_size("dp")
    n_tensor = lax.axis_size("tensor")
    rows_dev, d_dev = hidden.shape
    capacity, width = talker_in.shape
    kv_width = kv_grad.shape[1]
    slots = n_tensor * capacity
    share = rows_dev // n_tensor
    per_dev = kv_width // (n_dp * n_tensor)
    bf16, f32 = jnp.bfloat16, jnp.float32

    keys = 4 * GROUP_KEYS + 3 * NZ + 2
    hidden_rows, own_sum, swapped, weight_sums = pl.pallas_call(
        whole,
        out_shape=(
            jax.ShapeDtypeStruct((rows_dev, d_dev), bf16),
            jax.ShapeDtypeStruct((width // n_dp, d_dev), f32),
            jax.ShapeDtypeStruct((width // n_dp, d_dev), bf16),
            jax.ShapeDtypeStruct((8, width), f32),
        ),
        in_specs=[VMEM] * 5 + [ANY] * 2,
        out_specs=[VMEM] * 4,
        scratch_shapes=[
            pltpu.VMEM((n_tensor, capacity, width), bf16),
            pltpu.VMEM((n_tensor, capacity, kv_width), bf16),
            pltpu.VMEM((NZ, rows_dev, d_dev), bf16),
            pltpu.VMEM(kv_weight.shape, bf16),
            pltpu.VMEM(connector.shape, bf16),
            pltpu.VMEM((share, width), f32),
            pltpu.VMEM((share, width), bf16),
            pltpu.VMEM((NZ, 2, share, BLOCK), bf16),
            pltpu.VMEM((2, NZ, n_tensor, share, BLOCK), bf16),
            pltpu.VMEM((8, WINDOW, BLOCK), bf16),
            pltpu.VMEM((rows_dev, slots), bf16),
            pltpu.VMEM((rows_dev, width), bf16),
            pltpu.VMEM((rows_dev, kv_width), bf16),
            pltpu.VMEM((rows_dev, width), f32),
            pltpu.VMEM((n_dp * per_dev, rows_dev), bf16),
            pltpu.VMEM((NZ, 8, width), bf16),
            pltpu.VMEM((NZ, 8, width), bf16),
            pltpu.VMEM((BLOCK, d_dev), bf16),
            pltpu.VMEM((BLOCK, d_dev), bf16),
            pltpu.VMEM((8, width), f32),
            pltpu.VMEM((8, width), bf16),
            pltpu.VMEM((8, width), bf16),
            pltpu.VMEM((BLOCK, d_dev), f32),
            pltpu.VMEM((1, width), f32),
            pltpu.SemaphoreType.DMA((keys,)),
            pltpu.SemaphoreType.DMA((keys,)),
            pltpu.SemaphoreType.DMA((6,)),
        ],
        compiler_params=pltpu.CompilerParams(
            collective_id=0, has_side_effects=True, vmem_limit_bytes=60 * 1024 * 1024
        ),
    )(
        talker_in,
        kv_grad,
        hidden,
        norm_gain.reshape(width // 128, 128),
        routing.T,
        kv_weight,
        connector,
    )
    factor = 1.0 / math.sqrt(rows_dev * n_dp)
    hidden_grad, connector_grad, weight_grad = pl.pallas_call(
        functools.partial(close, factor),
        out_shape=(
            jax.ShapeDtypeStruct((rows_dev, d_dev), bf16),
            jax.ShapeDtypeStruct((width // n_dp, d_dev), f32),
            jax.ShapeDtypeStruct((per_dev, width), f32),
        ),
        in_specs=[VMEM] * 4,
        out_specs=[VMEM] * 3,
    )(hidden_rows, own_sum, swapped, weight_sums)
    return (hidden_grad, connector_grad.T, weight_grad.T)


def solution(mesh):
    return jax.shard_map(
        on_device,
        mesh=mesh,
        in_specs=(
            P("dp", "tensor"),
            P("tensor", None),
            P("dp", None),
            P(("dp", "tensor"), None),
            P(),
            P(),
            P(("dp", "tensor"), None),
        ),
        out_specs=(P("dp", "tensor"), P("tensor", "dp"), P(None, ("dp", "tensor"))),
        check_vma=False,
    )
```

```python
import functools
import math

import jax
import jax.numpy as jnp
from jax import lax
from jax.experimental import pallas as pl
from jax.experimental.pallas import tpu as pltpu
from jax.sharding import PartitionSpec as P

MESH = pl.DeviceIdType.MESH
CONTRACT_LAST = (((1,), (1,)), ((), ()))
CONTRACT_FIRST = (((0,), (0,)), ((), ()))

NZ = 8
NY = 4


class Place:
    def __init__(self):
        self.dp = lax.axis_index("dp")
        self.t = lax.axis_index("tensor")
        self.z = lax.rem(self.dp, NZ)
        self.xl = lax.div(self.dp, NZ)
        self.core = lax.rem(self.t, 2)
        self.y = lax.rem(lax.div(self.t, 2), NY)
        self.xh = lax.div(self.t, 2 * NY)

    def tensor(self, xh, y, core):
        return xh * (2 * NY) + lax.rem(y + NY, NY) * 2 + core

    def at_y(self, step):
        return (self.dp, self.tensor(self.xh, self.y + step, self.core))

    def at_z(self, step):
        return (self.xl * NZ + lax.rem(self.z + step + NZ, NZ), self.t)

    def across(self):
        return (self.dp, self.tensor(1 - self.xh, self.y, self.core))

    def sibling(self):
        return (self.dp, self.tensor(self.xh, self.y, 1 - self.core))


def greet(devices):
    barrier = pltpu.get_barrier_semaphore()
    for device in devices:
        pl.semaphore_signal(barrier, inc=1, device_id=device, device_id_type=MESH)
    pl.semaphore_wait(barrier, len(devices))


class Sends:
    def __init__(self, send_sems, recv_sems):
        self.send_sems, self.recv_sems = send_sems, recv_sems
        self.open = []

    def send(self, src, dst, key, device):
        copy = pltpu.make_async_remote_copy(
            src_ref=src,
            dst_ref=dst,
            send_sem=self.send_sems.at[key],
            recv_sem=self.recv_sems.at[key],
            device_id=device,
            device_id_type=MESH,
        )
        copy.start()
        self.open.append(copy)

    def arrived(self, dst, key, device):
        pltpu.make_async_remote_copy(
            src_ref=dst,
            dst_ref=dst,
            send_sem=self.send_sems.at[key],
            recv_sem=self.recv_sems.at[key],
            device_id=device,
            device_id_type=MESH,
        ).wait_recv()

    def drain(self):
        for copy in self.open:
            copy.wait_send()


GROUP_KEYS = 12 + 2 + 16


def key_y(direction, far, kind):
    return direction * 6 + far * 3 + kind


def key_x(half):
    return 12 + half


def key_s(hop, half):
    return 14 + hop * 2 + half


class GroupGather:
    def __init__(self, place, own, slot, sends, base):
        self.place, self.own, self.slot = place, own, slot
        self.sends, self.base = sends, base

    def block(self, far, step):
        p = self.place
        return p.tensor(1 - p.xh if far else p.xh, p.y + step, p.core)

    def twin(self, far, step):
        p = self.place
        return p.tensor(1 - p.xh if far else p.xh, p.y + step, 1 - p.core)

    def hop(self, far, step):
        return far * 4 + step % 4

    def share(self, src, far, step, half):
        self.sends.send(
            src,
            self.slot(self.block(far, step), half),
            self.base + key_s(self.hop(far, step), half),
            self.place.sibling(),
        )

    def to_y(self, src, far, half, direction):
        step = 1 if direction == 0 else -1
        self.sends.send(
            src,
            self.slot(self.block(far, 0), half),
            self.base + key_y(direction, far, half),
            self.place.at_y(step),
        )

    def start(self, halves=(0, 1)):
        for half in halves:
            self.to_y(self.own(half), 0, half, half)
            self.to_y(self.own(half), 0, half, 1 - half)
            self.across_first(half)
        for half in halves:
            self.share(self.own(half), 0, 0, half)

    def across_first(self, half):
        self.sends.send(
            self.own(half),
            self.slot(self.block(0, 0), half),
            self.base + key_x(half),
            self.place.across(),
        )

    def take_x(self, half):
        dst = self.slot(self.block(1, 0), half)
        self.sends.arrived(dst, self.base + key_x(half), self.place.across())
        self.to_y(dst, 1, half, 0)
        self.to_y(dst, 1, half, 1)
        self.share(dst, 1, 0, half)

    def take_y(self, far, half, direction):
        step = -1 if direction == 0 else 1
        dst = self.slot(self.block(far, step), half)
        self.sends.arrived(
            dst, self.base + key_y(direction, far, half), self.place.at_y(step)
        )
        if half == direction:
            self.sends.send(
                dst,
                dst,
                self.base + key_y(direction, far, 2),
                self.place.at_y(-step),
            )
        self.share(dst, far, step, half)

    def take_far(self, far, direction):
        step = -1 if direction == 0 else 1
        half = direction
        dst = self.slot(self.block(far, 2 * step), half)
        self.sends.arrived(
            dst, self.base + key_y(direction, far, 2), self.place.at_y(step)
        )
        self.share(dst, far, 2, half)

    def take_shared(self, halves=(0, 1)):
        for far in (0, 1):
            for step in (0, 1, 2, 3):
                for half in halves:
                    self.sends.arrived(
                        self.slot(self.twin(far, step), half),
                        self.base + key_s(self.hop(far, step), half),
                        self.place.sibling(),
                    )


class GatherFromY(GroupGather):
    def across_first(self, half):
        self.to_x(self.own(half), 0, half)

    def to_x(self, src, step, half):
        self.sends.send(
            src,
            self.slot(self.block(0, step), half),
            self.base + key_from_y(step, half),
            self.place.across(),
        )

    def take_y(self, far, half, direction):
        super().take_y(0, half, direction)
        step = -1 if direction == 0 else 1
        self.to_x(self.slot(self.block(0, step), half), step, half)

    def take_far(self, far, direction):
        super().take_far(0, direction)
        self.to_x(self.slot(self.block(0, 2), direction), 2, direction)

    def take_x(self, step, half):
        dst = self.slot(self.block(1, step), half)
        self.sends.arrived(dst, self.base + key_from_y(step, half), self.place.across())
        self.share(dst, 1, step, half)


def key_from_y(step, half):
    return (3, 4, 5, 9, 10, 11, 12, 13)[(step % 4) * 2 + half]


TILE = 512
BLOCK = 256
WINDOW = 384


def onehot(rows):
    return jnp.where(rows, 1.0, 0.0).astype(jnp.bfloat16)


def dot(a, b, contract):
    return lax.dot_general(a, b, (contract, ((), ())), preferred_element_type=jnp.float32)


NN = ((1,), (0,))
NT = ((1,), (1,))
TN = ((0,), (0,))


def whole(
    talker_ref, kv_ref, hidden_ref, gain_rows_ref, route_ref, weight_any, connector_any,
    hidden_grad_ref, own_sum_ref, swapped_ref, weight_sums_ref,
    talkers, kvs, hiddens, weight, connector,
    local_rows, local_grad, packed, blocks, shifts, pick, rows, kv_rows, back, columns, terms, terms_in,
    away, away_in, sums, sums_out, sums_in, total, gain_ref, send_sems, recv_sems, own_sems,
):
    bf16, f32 = jnp.bfloat16, jnp.float32
    place = Place()
    width = talker_ref.shape[1]
    tiles = width // TILE
    capacity = talker_ref.shape[0]
    n_tensor = talkers.shape[0]
    slots = n_tensor * capacity
    rows_dev = hidden_ref.shape[0]
    share = rows_dev // n_tensor
    piece_rows = own_sum_ref.shape[0]
    loads = [
        pltpu.make_async_copy(weight_any, weight, own_sems.at[0]),
        pltpu.make_async_copy(connector_any, connector, own_sems.at[1]),
    ]
    for load in loads:
        load.start()
    over_x = (lax.rem(place.dp + NZ, 2 * NZ), place.t)
    greet(
        [place.at_z(step) for step in range(1, NZ)]
        + [place.at_y(1), place.at_y(-1), place.across(), place.sibling(), over_x]
    )
    sends = Sends(send_sems, recv_sems)
    half_rows = capacity // 2
    half_hidden = rows_dev // 2
    kept = [
        pltpu.make_async_copy(talker_ref, talkers.at[place.t], own_sems.at[2]),
        pltpu.make_async_copy(kv_ref, kvs.at[place.t], own_sems.at[3]),
        pltpu.make_async_copy(hidden_ref, hiddens.at[place.z], own_sems.at[4]),
    ]

    def tile_of(i):
        return pl.ds(pl.multiple_of(i * TILE, TILE), TILE)

    def gather(kind, own_ref, where, base):
        return kind(
            place,
            lambda half: own_ref.at[pl.ds(half * half_rows, half_rows)],
            lambda block, half: where.at[block, pl.ds(half * half_rows, half_rows)],
            sends,
            base,
        )

    wide = gather(GroupGather, talker_ref, talkers, 0)
    thin = gather(GatherFromY, kv_ref, kvs, GROUP_KEYS)

    def block_slot(block, half):
        return blocks.at[lax.rem(1 - place.xl + half, 2), :, block]

    def own_block(half):
        return block_slot(place.t, half)

    theirs = GroupGather(place, own_block, block_slot, sends, 2 * GROUP_KEYS)
    ours = GatherFromY(place, own_block, block_slot, sends, 3 * GROUP_KEYS)
    z_base = 4 * GROUP_KEYS
    packed_base = z_base + NZ
    terms_base = packed_base + NZ
    x_base = terms_base + NZ

    def z_at(step):
        return lax.rem(place.z + step + NZ, NZ)

    def z_slot(step, part=None):
        slot = hiddens.at[z_at(step)]
        if part is None:
            return slot
        return slot.at[pl.ds(part * half_hidden, half_hidden)]

    def pass_z(hop):
        for direction, step in ((0, -1), (1, 1)):
            if hop:
                sends.arrived(z_slot(hop * step), z_base + direction * 4 + hop - 1, place.at_z(step))
            part = direction if hop == 3 else None
            src = z_slot(hop * step, part) if hop else hidden_ref
            sends.send(
                src, z_slot(hop * step, part), z_base + direction * 4 + hop, place.at_z(-step)
            )

    def to_all_z(src, dst, base):
        for step in (1, 7, 2, 6, 3, 5, 4):
            sends.send(src(step), dst, base + step, place.at_z(step))

    def from_all_z(dst, base):
        for step in (1, 7, 2, 6, 3, 5, 4):
            sends.arrived(dst(-step), base + step, place.at_z(-step))

    def number_rows():
        route = route_ref[...]
        shard = lax.broadcasted_iota(jnp.int32, (n_tensor, rows_dev), 0)
        named = shard == route
        earlier = lax.broadcasted_iota(jnp.int32, (rows_dev, rows_dev), 0)
        later = lax.broadcasted_iota(jnp.int32, (rows_dev, rows_dev), 1)
        before = dot(onehot(named), onehot(earlier < later), NN)
        rank = jnp.sum(jnp.where(named, before, 0.0), axis=0, keepdims=True)
        slot = route * capacity + rank.astype(jnp.int32)
        slot_at = lax.broadcasted_iota(jnp.int32, (slots, rows_dev), 0)
        same = onehot(earlier == later)
        pick[...] = dot(same, onehot(slot_at == slot), NT).astype(bf16)
        lanes = gain_rows_ref.shape[1]
        for i in range(gain_rows_ref.shape[0]):
            gain_ref[:, i * lanes : (i + 1) * lanes] = gain_rows_ref[i : i + 1, :]

    def own_rows():
        mine = pl.ds(pl.multiple_of(place.t * share, share), share)

        def first(i, carry):
            squares, products = carry
            tile = tile_of(i)
            inputs = dot(pick[mine, :], talkers[:, :, tile].reshape(slots, TILE), NN)
            local_rows[:, tile] = inputs
            gained = back[mine, tile]
            return (
                squares + jnp.sum(inputs * inputs, axis=1, keepdims=True),
                products + jnp.sum(gained * inputs, axis=1, keepdims=True),
            )

        zero = jnp.zeros((share, 1), f32)
        squares, products = lax.fori_loop(0, tiles, first, (zero, zero))
        inv_rms = lax.rsqrt(squares / width + 1e-06)
        mean = products * inv_rms / width

        def second(i, carry):
            tile = tile_of(i)
            scaled = local_rows[:, tile] * inv_rms
            local_grad[:, tile] = (inv_rms * (back[mine, tile] - scaled * mean)).astype(bf16)
            return carry

        lax.fori_loop(0, tiles, second, 0)
        for index in range(2 * NZ):
            start, kind = cuts[index]
            packed[index % NZ, index // NZ] = dot(
                local_grad[:, start : start + WINDOW], shifts[kind], NN
            ).astype(bf16)

    def make_shifts():
        window_at = lax.broadcasted_iota(jnp.int32, (WINDOW, BLOCK), 0)
        wanted = lax.broadcasted_iota(jnp.int32, (WINDOW, BLOCK), 1)
        for kind, offset in enumerate(offsets):
            shifts[kind] = onehot((window_at == wanted + offset) & (wanted < piece))

    def pick_kv():
        kv_all = kvs[...].reshape(slots, kvs.shape[2])
        kv_rows[...] = dot(pick[...], kv_all, NN).astype(bf16)
        at = lax.broadcasted_iota(jnp.int32, columns_shape, 0)
        col = lax.broadcasted_iota(jnp.int32, columns_shape, 1)
        dp = ((at >> 2) & 1) * NZ + (at >> 3)
        chosen = onehot(col == (dp * n_tensor + place.t) * 4 + (at & 3))
        columns[...] = dot(chosen, kv_rows[...], NT).astype(bf16)

    def make_back(first, last):
        def one(i, carry):
            tile = tile_of(i)
            back[:, tile] = gain_ref[:, tile] * dot(kv_rows[...], weight[tile, :], NT)
            return carry

        lax.fori_loop(first, last, one, 0)

    def pick_rows():
        def one(i, carry):
            squares, products = carry
            tile = tile_of(i)
            inputs = dot(pick[...], talkers[:, :, tile].reshape(slots, TILE), NN)
            rows[:, tile] = inputs.astype(bf16)
            return (
                squares + jnp.sum(inputs * inputs, axis=1, keepdims=True),
                products + jnp.sum(back[:, tile] * inputs, axis=1, keepdims=True),
            )

        zero = jnp.zeros((rows_dev, 1), f32)
        squares, products = lax.fori_loop(0, tiles, one, (zero, zero))
        return lax.rsqrt(squares / width + 1e-06), products

    piece = width // (2 * NZ)
    starts = [min(i * piece // 128 * 128, width - WINDOW) for i in range(2 * NZ)]
    offsets = sorted({i * piece - start for i, start in enumerate(starts)})
    cuts = [(start, offsets.index(i * piece - start)) for i, start in enumerate(starts)]
    columns_shape = (terms.shape[0] * terms.shape[1], kv_ref.shape[1])

    def make_terms(inv_rms):
        def one(i, carry):
            tile = tile_of(i)
            normed = ((rows[:, tile].astype(f32) * inv_rms) * gain_ref[:, tile]).astype(bf16)
            term = dot(columns[...], normed, NN)
            for at in range(NZ):
                terms[at, :, tile] = term[at * 8 : (at + 1) * 8].astype(bf16)
            return carry

        lax.fori_loop(0, tiles, one, 0)

    def make_hidden_grad(inv_rms, products):
        mean = products * inv_rms / width
        total[...] = jnp.zeros_like(total)

        def one(i, carry):
            tile = tile_of(i)
            scaled = rows[:, tile].astype(f32) * inv_rms
            grad = (inv_rms * (back[:, tile] - scaled * mean)).astype(bf16)
            total[...] += dot(grad, connector[:, tile], NT)
            return carry

        lax.fori_loop(0, tiles, one, 0)
        hidden_grad_ref[...] = total[...].astype(bf16)

    def connector_part(block):
        part = NZ // 4
        total[...] = jnp.zeros_like(total)

        def one(i, carry):
            at = pl.ds(i * part, part)
            lhs = blocks[block, at].reshape(part * rows_dev, BLOCK)
            rhs = hiddens[at].reshape(part * rows_dev, hiddens.shape[2])
            total[...] += dot(lhs, rhs, TN)
            return carry

        lax.fori_loop(0, 4, one, 0)

    wide.start()
    thin.start()
    pass_z(0)
    for copy in kept:
        copy.start()
    number_rows()
    make_shifts()
    for direction in (0, 1):
        wide.take_y(0, direction, direction)
    wide.take_x(0)
    for direction in (0, 1):
        wide.take_y(0, 1 - direction, direction)
    wide.take_x(1)
    pass_z(1)
    for half in (0, 1):
        for direction in (half, 1 - half):
            thin.take_y(0, half, direction)
    for direction in (0, 1):
        wide.take_far(0, direction)
        thin.take_far(0, direction)
    for direction in (0, 1):
        wide.take_y(1, direction, direction)
    pass_z(2)
    for direction in (0, 1):
        wide.take_y(1, 1 - direction, direction)
    for step in (0, 1, -1, 2):
        for half in (0, 1):
            thin.take_x(step, half)
    thin.take_shared()
    kept[1].wait()
    pick_kv()
    loads[0].wait()
    make_back(0, 3)
    for direction in (0, 1):
        wide.take_far(1, direction)
    make_back(3, tiles)
    wide.take_shared()
    kept[0].wait()
    own_rows()
    own_packed = pltpu.make_async_copy(
        packed.at[place.z], blocks.at[:, place.z, place.t], own_sems.at[5]
    )
    own_packed.start()
    to_all_z(lambda step: packed.at[z_at(step)], blocks.at[:, place.z, place.t], packed_base)
    pass_z(3)
    inv_rms, products = pick_rows()
    make_terms(inv_rms)
    from_all_z(lambda step: blocks.at[:, z_at(step), place.t], packed_base)
    own_packed.wait()
    theirs.start((0,))
    ours.start((1,))
    to_all_z(lambda step: terms.at[z_at(step)], terms_in.at[place.z], terms_base)
    ours.take_y(0, 1, 1)
    theirs.take_y(0, 0, 0)
    ours.take_y(0, 1, 0)
    theirs.take_y(0, 0, 1)
    theirs.take_x(0)
    ours.take_far(0, 1)
    ours.take_x(0, 1)
    theirs.take_far(0, 0)
    theirs.take_y(1, 0, 0)
    theirs.take_y(1, 0, 1)
    for step in (1, -1):
        ours.take_x(step, 1)
    theirs.take_far(1, 0)
    ours.take_x(2, 1)
    for direction, step in ((0, -1), (1, 1)):
        sends.arrived(z_slot(4 * step, direction), z_base + direction * 4 + 3, place.at_z(step))
    kept[2].wait()
    theirs.take_shared((0,))
    connector_part(1 - place.xl)
    away[...] = total[...].astype(bf16)
    sends.send(
        away.at[pl.ds(0, piece_rows)], away_in.at[pl.ds(0, piece_rows)], x_base, over_x
    )
    from_all_z(lambda step: terms_in.at[z_at(step)], terms_base)
    terms_in[place.z] = terms[place.z]

    def add_up(i, carry):
        tile = tile_of(i)
        added = jnp.sum(terms_in[:, :, tile].astype(f32), axis=0)
        sums[:, tile] = added
        sums_out[:, tile] = added.astype(bf16)
        return carry

    lax.fori_loop(0, tiles, add_up, 0)
    sends.send(sums_out, sums_in, x_base + 1, over_x)
    loads[1].wait()
    make_hidden_grad(inv_rms, products)
    ours.take_shared((1,))
    connector_part(place.xl)
    own_sum_ref[...] = total[0:piece_rows, :]
    sends.arrived(sums_in, x_base + 1, over_x)
    weight_sums_ref[...] = sums[...] + sums_in[...].astype(f32)
    sends.arrived(away_in.at[pl.ds(0, piece_rows)], x_base, over_x)
    swapped_ref[...] = away_in[0:piece_rows, :]
    sends.drain()


def close(factor, hidden_ref, own_ref, swapped_ref, sums_ref, hidden_grad_ref, connector_grad_ref, weight_grad_ref):
    hidden_grad_ref[...] = hidden_ref[...]
    connector_grad_ref[...] = (own_ref[...] + swapped_ref[...].astype(jnp.float32)) * factor
    sums = sums_ref[...]
    mine = jnp.where(lax.axis_index("dp") < NZ, sums[0:4], sums[4:8])
    weight_grad_ref[...] = mine * factor


VMEM = pl.BlockSpec(memory_space=pltpu.VMEM)
ANY = pl.BlockSpec(memory_space=pl.ANY)


def on_device(hidden, connector, routing, talker_in, norm_gain, kv_weight, kv_grad):
    n_dp = lax.axis_size("dp")
    n_tensor = lax.axis_size("tensor")
    rows_dev, d_dev = hidden.shape
    capacity, width = talker_in.shape
    kv_width = kv_grad.shape[1]
    slots = n_tensor * capacity
    share = rows_dev // n_tensor
    per_dev = kv_width // (n_dp * n_tensor)
    bf16, f32 = jnp.bfloat16, jnp.float32

    keys = 4 * GROUP_KEYS + 3 * NZ + 2
    hidden_rows, own_sum, swapped, weight_sums = pl.pallas_call(
        whole,
        out_shape=(
            jax.ShapeDtypeStruct((rows_dev, d_dev), bf16),
            jax.ShapeDtypeStruct((width // n_dp, d_dev), f32),
            jax.ShapeDtypeStruct((width // n_dp, d_dev), bf16),
            jax.ShapeDtypeStruct((8, width), f32),
        ),
        in_specs=[VMEM] * 5 + [ANY] * 2,
        out_specs=[VMEM] * 4,
        scratch_shapes=[
            pltpu.VMEM((n_tensor, capacity, width), bf16),
            pltpu.VMEM((n_tensor, capacity, kv_width), bf16),
            pltpu.VMEM((NZ, rows_dev, d_dev), bf16),
            pltpu.VMEM(kv_weight.shape, bf16),
            pltpu.VMEM(connector.shape, bf16),
            pltpu.VMEM((share, width), f32),
            pltpu.VMEM((share, width), bf16),
            pltpu.VMEM((NZ, 2, share, BLOCK), bf16),
            pltpu.VMEM((2, NZ, n_tensor, share, BLOCK), bf16),
            pltpu.VMEM((8, WINDOW, BLOCK), bf16),
            pltpu.VMEM((rows_dev, slots), bf16),
            pltpu.VMEM((rows_dev, width), bf16),
            pltpu.VMEM((rows_dev, kv_width), bf16),
            pltpu.VMEM((rows_dev, width), f32),
            pltpu.VMEM((n_dp * per_dev, rows_dev), bf16),
            pltpu.VMEM((NZ, 8, width), bf16),
            pltpu.VMEM((NZ, 8, width), bf16),
            pltpu.VMEM((BLOCK, d_dev), bf16),
            pltpu.VMEM((BLOCK, d_dev), bf16),
            pltpu.VMEM((8, width), f32),
            pltpu.VMEM((8, width), bf16),
            pltpu.VMEM((8, width), bf16),
            pltpu.VMEM((BLOCK, d_dev), f32),
            pltpu.VMEM((1, width), f32),
            pltpu.SemaphoreType.DMA((keys,)),
            pltpu.SemaphoreType.DMA((keys,)),
            pltpu.SemaphoreType.DMA((6,)),
        ],
        compiler_params=pltpu.CompilerParams(
            collective_id=0, has_side_effects=True, vmem_limit_bytes=60 * 1024 * 1024
        ),
    )(
        talker_in,
        kv_grad,
        hidden,
        norm_gain.reshape(width // 128, 128),
        routing.T,
        kv_weight,
        connector,
    )
    factor = 1.0 / math.sqrt(rows_dev * n_dp)
    hidden_grad, connector_grad, weight_grad = pl.pallas_call(
        functools.partial(close, factor),
        out_shape=(
            jax.ShapeDtypeStruct((rows_dev, d_dev), bf16),
            jax.ShapeDtypeStruct((width // n_dp, d_dev), f32),
            jax.ShapeDtypeStruct((per_dev, width), f32),
        ),
        in_specs=[VMEM] * 4,
        out_specs=[VMEM] * 3,
    )(hidden_rows, own_sum, swapped, weight_sums)
    return (hidden_grad, connector_grad.T, weight_grad.T)


def solution(mesh):
    return jax.shard_map(
        on_device,
        mesh=mesh,
        in_specs=(
            P("dp", "tensor"),
            P("tensor", None),
            P("dp", None),
            P(("dp", "tensor"), None),
            P(),
            P(),
            P(("dp", "tensor"), None),
        ),
        out_specs=(P("dp", "tensor"), P("tensor", "dp"), P(None, ("dp", "tensor"))),
        check_vma=False,
    )
```

```python
import functools
import math

import jax
import jax.numpy as jnp
from jax import lax
from jax.experimental import pallas as pl
from jax.experimental.pallas import tpu as pltpu
from jax.sharding import PartitionSpec as P

MESH = pl.DeviceIdType.MESH
CONTRACT_LAST = (((1,), (1,)), ((), ()))
CONTRACT_FIRST = (((0,), (0,)), ((), ()))

NZ = 8
NY = 4


class Place:
    def __init__(self):
        self.dp = lax.axis_index("dp")
        self.t = lax.axis_index("tensor")
        self.z = lax.rem(self.dp, NZ)
        self.xl = lax.div(self.dp, NZ)
        self.core = lax.rem(self.t, 2)
        self.y = lax.rem(lax.div(self.t, 2), NY)
        self.xh = lax.div(self.t, 2 * NY)

    def tensor(self, xh, y, core):
        return xh * (2 * NY) + lax.rem(y + NY, NY) * 2 + core

    def at_y(self, step):
        return (self.dp, self.tensor(self.xh, self.y + step, self.core))

    def at_z(self, step):
        return (self.xl * NZ + lax.rem(self.z + step + NZ, NZ), self.t)

    def across(self):
        return (self.dp, self.tensor(1 - self.xh, self.y, self.core))

    def sibling(self):
        return (self.dp, self.tensor(self.xh, self.y, 1 - self.core))


def greet(devices):
    barrier = pltpu.get_barrier_semaphore()
    for device in devices:
        pl.semaphore_signal(barrier, inc=1, device_id=device, device_id_type=MESH)
    pl.semaphore_wait(barrier, len(devices))


class Sends:
    def __init__(self, send_sems, recv_sems):
        self.send_sems, self.recv_sems = send_sems, recv_sems
        self.open = []

    def send(self, src, dst, key, device):
        copy = pltpu.make_async_remote_copy(
            src_ref=src,
            dst_ref=dst,
            send_sem=self.send_sems.at[key],
            recv_sem=self.recv_sems.at[key],
            device_id=device,
            device_id_type=MESH,
        )
        copy.start()
        self.open.append(copy)

    def arrived(self, dst, key, device):
        pltpu.make_async_remote_copy(
            src_ref=dst,
            dst_ref=dst,
            send_sem=self.send_sems.at[key],
            recv_sem=self.recv_sems.at[key],
            device_id=device,
            device_id_type=MESH,
        ).wait_recv()

    def drain(self):
        for copy in self.open:
            copy.wait_send()


GROUP_KEYS = 12 + 2 + 16


def key_y(direction, far, kind):
    return direction * 6 + far * 3 + kind


def key_x(half):
    return 12 + half


def key_s(hop, half):
    return 14 + hop * 2 + half


class GroupGather:
    def __init__(self, place, own, slot, sends, base):
        self.place, self.own, self.slot = place, own, slot
        self.sends, self.base = sends, base

    def block(self, far, step):
        p = self.place
        return p.tensor(1 - p.xh if far else p.xh, p.y + step, p.core)

    def twin(self, far, step):
        p = self.place
        return p.tensor(1 - p.xh if far else p.xh, p.y + step, 1 - p.core)

    def hop(self, far, step):
        return far * 4 + step % 4

    def share(self, src, far, step, half):
        self.sends.send(
            src,
            self.slot(self.block(far, step), half),
            self.base + key_s(self.hop(far, step), half),
            self.place.sibling(),
        )

    def to_y(self, src, far, half, direction):
        step = 1 if direction == 0 else -1
        self.sends.send(
            src,
            self.slot(self.block(far, 0), half),
            self.base + key_y(direction, far, half),
            self.place.at_y(step),
        )

    def start(self, halves=(0, 1)):
        for half in halves:
            self.to_y(self.own(half), 0, half, half)
            self.to_y(self.own(half), 0, half, 1 - half)
            self.across_first(half)
        for half in halves:
            self.share(self.own(half), 0, 0, half)

    def across_first(self, half):
        self.sends.send(
            self.own(half),
            self.slot(self.block(0, 0), half),
            self.base + key_x(half),
            self.place.across(),
        )

    def take_x(self, half):
        dst = self.slot(self.block(1, 0), half)
        self.sends.arrived(dst, self.base + key_x(half), self.place.across())
        self.to_y(dst, 1, half, 0)
        self.to_y(dst, 1, half, 1)
        self.share(dst, 1, 0, half)

    def take_y(self, far, half, direction):
        step = -1 if direction == 0 else 1
        dst = self.slot(self.block(far, step), half)
        self.sends.arrived(
            dst, self.base + key_y(direction, far, half), self.place.at_y(step)
        )
        if half == direction:
            self.sends.send(
                dst,
                dst,
                self.base + key_y(direction, far, 2),
                self.place.at_y(-step),
            )
        self.share(dst, far, step, half)

    def take_far(self, far, direction):
        step = -1 if direction == 0 else 1
        half = direction
        dst = self.slot(self.block(far, 2 * step), half)
        self.sends.arrived(
            dst, self.base + key_y(direction, far, 2), self.place.at_y(step)
        )
        self.share(dst, far, 2, half)

    def take_shared(self, halves=(0, 1)):
        for far in (0, 1):
            for step in (0, 1, 2, 3):
                for half in halves:
                    self.sends.arrived(
                        self.slot(self.twin(far, step), half),
                        self.base + key_s(self.hop(far, step), half),
                        self.place.sibling(),
                    )


class GatherFromY(GroupGather):
    def across_first(self, half):
        self.to_x(self.own(half), 0, half)

    def to_x(self, src, step, half):
        self.sends.send(
            src,
            self.slot(self.block(0, step), half),
            self.base + key_from_y(step, half),
            self.place.across(),
        )

    def take_y(self, far, half, direction):
        super().take_y(0, half, direction)
        step = -1 if direction == 0 else 1
        self.to_x(self.slot(self.block(0, step), half), step, half)

    def take_far(self, far, direction):
        super().take_far(0, direction)
        self.to_x(self.slot(self.block(0, 2), direction), 2, direction)

    def take_x(self, step, half):
        dst = self.slot(self.block(1, step), half)
        self.sends.arrived(dst, self.base + key_from_y(step, half), self.place.across())
        self.share(dst, 1, step, half)


def key_from_y(step, half):
    return (3, 4, 5, 9, 10, 11, 12, 13)[(step % 4) * 2 + half]


TILE = 512
BLOCK = 256
WINDOW = 384


def onehot(rows):
    return jnp.where(rows, 1.0, 0.0).astype(jnp.bfloat16)


def dot(a, b, contract):
    return lax.dot_general(a, b, (contract, ((), ())), preferred_element_type=jnp.float32)


NN = ((1,), (0,))
NT = ((1,), (1,))
TN = ((0,), (0,))


def whole(
    talker_ref, kv_ref, hidden_ref, gain_rows_ref, route_ref, weight_any, connector_any,
    hidden_grad_ref, own_sum_ref, swapped_ref, weight_sums_ref,
    talkers, kvs, hiddens, weight, connector,
    local_rows, local_back, local_grad, packed, blocks, shifts, pick, rows, kv_rows, back, columns, terms, terms_in,
    away, away_in, sums, sums_out, sums_in, total, gain_ref, send_sems, recv_sems, own_sems,
):
    bf16, f32 = jnp.bfloat16, jnp.float32
    place = Place()
    width = talker_ref.shape[1]
    tiles = width // TILE
    capacity = talker_ref.shape[0]
    n_tensor = talkers.shape[0]
    slots = n_tensor * capacity
    rows_dev = hidden_ref.shape[0]
    share = rows_dev // n_tensor
    piece_rows = own_sum_ref.shape[0]
    loads = [
        pltpu.make_async_copy(weight_any, weight, own_sems.at[0]),
        pltpu.make_async_copy(connector_any, connector, own_sems.at[1]),
    ]
    for load in loads:
        load.start()
    over_x = (lax.rem(place.dp + NZ, 2 * NZ), place.t)
    greet(
        [place.at_z(step) for step in range(1, NZ)]
        + [place.at_y(1), place.at_y(-1), place.across(), place.sibling(), over_x]
    )
    sends = Sends(send_sems, recv_sems)
    half_rows = capacity // 2
    half_hidden = rows_dev // 2
    kept = [
        pltpu.make_async_copy(talker_ref, talkers.at[place.t], own_sems.at[2]),
        pltpu.make_async_copy(kv_ref, kvs.at[place.t], own_sems.at[3]),
        pltpu.make_async_copy(hidden_ref, hiddens.at[place.z], own_sems.at[4]),
    ]

    def tile_of(i):
        return pl.ds(pl.multiple_of(i * TILE, TILE), TILE)

    def gather(kind, own_ref, where, base):
        return kind(
            place,
            lambda half: own_ref.at[pl.ds(half * half_rows, half_rows)],
            lambda block, half: where.at[block, pl.ds(half * half_rows, half_rows)],
            sends,
            base,
        )

    wide = gather(GroupGather, talker_ref, talkers, 0)
    thin = gather(GatherFromY, kv_ref, kvs, GROUP_KEYS)

    def block_slot(block, half):
        return blocks.at[lax.rem(1 - place.xl + half, 2), :, block]

    def own_block(half):
        return block_slot(place.t, half)

    theirs = GroupGather(place, own_block, block_slot, sends, 2 * GROUP_KEYS)
    ours = GatherFromY(place, own_block, block_slot, sends, 3 * GROUP_KEYS)
    z_base = 4 * GROUP_KEYS
    packed_base = z_base + NZ
    terms_base = packed_base + NZ
    x_base = terms_base + NZ

    def z_at(step):
        return lax.rem(place.z + step + NZ, NZ)

    def z_slot(step, part=None):
        slot = hiddens.at[z_at(step)]
        if part is None:
            return slot
        return slot.at[pl.ds(part * half_hidden, half_hidden)]

    def pass_z(hop):
        for direction, step in ((0, -1), (1, 1)):
            if hop:
                sends.arrived(z_slot(hop * step), z_base + direction * 4 + hop - 1, place.at_z(step))
            part = direction if hop == 3 else None
            src = z_slot(hop * step, part) if hop else hidden_ref
            sends.send(
                src, z_slot(hop * step, part), z_base + direction * 4 + hop, place.at_z(-step)
            )

    def to_all_z(src, dst, base):
        for step in (1, 7, 2, 6, 3, 5, 4):
            sends.send(src(step), dst, base + step, place.at_z(step))

    def from_all_z(dst, base):
        for step in (1, 7, 2, 6, 3, 5, 4):
            sends.arrived(dst(-step), base + step, place.at_z(-step))

    def number_rows():
        route = route_ref[...]
        shard = lax.broadcasted_iota(jnp.int32, (n_tensor, rows_dev), 0)
        named = shard == route
        earlier = lax.broadcasted_iota(jnp.int32, (rows_dev, rows_dev), 0)
        later = lax.broadcasted_iota(jnp.int32, (rows_dev, rows_dev), 1)
        before = dot(onehot(named), onehot(earlier < later), NN)
        rank = jnp.sum(jnp.where(named, before, 0.0), axis=0, keepdims=True)
        slot = route * capacity + rank.astype(jnp.int32)
        slot_at = lax.broadcasted_iota(jnp.int32, (slots, rows_dev), 0)
        same = onehot(earlier == later)
        pick[...] = dot(same, onehot(slot_at == slot), NT).astype(bf16)
        lanes = gain_rows_ref.shape[1]
        for i in range(gain_rows_ref.shape[0]):
            gain_ref[:, i * lanes : (i + 1) * lanes] = gain_rows_ref[i : i + 1, :]

    def own_rows():
        mine = pl.ds(pl.multiple_of(place.t * share, share), share)
        kv_all = kvs[...].reshape(slots, kvs.shape[2])
        kv_rows[...] = dot(pick[...], kv_all, NN).astype(bf16)

        def first(i, carry):
            squares, products = carry
            tile = tile_of(i)
            inputs = dot(pick[mine, :], talkers[:, :, tile].reshape(slots, TILE), NN)
            local_rows[:, tile] = inputs
            gained = gain_ref[:, tile] * dot(kv_rows[mine, :], weight[tile, :], NT)
            local_back[:, tile] = gained
            return (
                squares + jnp.sum(inputs * inputs, axis=1, keepdims=True),
                products + jnp.sum(gained * inputs, axis=1, keepdims=True),
            )

        zero = jnp.zeros((share, 1), f32)
        squares, products = lax.fori_loop(0, tiles, first, (zero, zero))
        inv_rms = lax.rsqrt(squares / width + 1e-06)
        mean = products * inv_rms / width

        def second(i, carry):
            tile = tile_of(i)
            scaled = local_rows[:, tile] * inv_rms
            local_grad[:, tile] = (inv_rms * (local_back[:, tile] - scaled * mean)).astype(bf16)
            return carry

        lax.fori_loop(0, tiles, second, 0)
        for index in range(2 * NZ):
            start, kind = cuts[index]
            packed[index % NZ, index // NZ] = dot(
                local_grad[:, start : start + WINDOW], shifts[kind], NN
            ).astype(bf16)

    def make_shifts():
        window_at = lax.broadcasted_iota(jnp.int32, (WINDOW, BLOCK), 0)
        wanted = lax.broadcasted_iota(jnp.int32, (WINDOW, BLOCK), 1)
        for kind, offset in enumerate(offsets):
            shifts[kind] = onehot((window_at == wanted + offset) & (wanted < piece))

    def pick_rows():
        at = lax.broadcasted_iota(jnp.int32, columns_shape, 0)
        col = lax.broadcasted_iota(jnp.int32, columns_shape, 1)
        dp = ((at >> 2) & 1) * NZ + (at >> 3)
        chosen = onehot(col == (dp * n_tensor + place.t) * 4 + (at & 3))
        columns[...] = dot(chosen, kv_rows[...], NT).astype(bf16)

        def one(i, squares):
            tile = tile_of(i)
            inputs = dot(pick[...], talkers[:, :, tile].reshape(slots, TILE), NN)
            rows[:, tile] = inputs.astype(bf16)
            return squares + jnp.sum(inputs * inputs, axis=1, keepdims=True)

        squares = lax.fori_loop(0, tiles, one, jnp.zeros((rows_dev, 1), f32))
        return lax.rsqrt(squares / width + 1e-06)

    piece = width // (2 * NZ)
    starts = [min(i * piece // 128 * 128, width - WINDOW) for i in range(2 * NZ)]
    offsets = sorted({i * piece - start for i, start in enumerate(starts)})
    cuts = [(start, offsets.index(i * piece - start)) for i, start in enumerate(starts)]
    columns_shape = (terms.shape[0] * terms.shape[1], kv_ref.shape[1])

    def make_terms(inv_rms):
        def one(i, carry):
            tile = tile_of(i)
            normed = ((rows[:, tile].astype(f32) * inv_rms) * gain_ref[:, tile]).astype(bf16)
            term = dot(columns[...], normed, NN)
            for at in range(NZ):
                terms[at, :, tile] = term[at * 8 : (at + 1) * 8].astype(bf16)
            return carry

        lax.fori_loop(0, tiles, one, 0)

    def make_back(first, last, products):
        def one(i, products):
            tile = tile_of(i)
            gained = gain_ref[:, tile] * dot(kv_rows[...], weight[tile, :], NT)
            back[:, tile] = gained
            return products + jnp.sum(gained * rows[:, tile].astype(f32), axis=1, keepdims=True)

        return lax.fori_loop(first, last, one, products)

    def make_hidden_grad(inv_rms, products):
        mean = products * inv_rms / width
        total[...] = jnp.zeros_like(total)

        def one(i, carry):
            tile = tile_of(i)
            scaled = rows[:, tile].astype(f32) * inv_rms
            grad = (inv_rms * (back[:, tile] - scaled * mean)).astype(bf16)
            total[...] += dot(grad, connector[:, tile], NT)
            return carry

        lax.fori_loop(0, tiles, one, 0)
        hidden_grad_ref[...] = total[...].astype(bf16)

    def connector_part(block):
        part = NZ // 4
        total[...] = jnp.zeros_like(total)

        def one(i, carry):
            at = pl.ds(i * part, part)
            lhs = blocks[block, at].reshape(part * rows_dev, BLOCK)
            rhs = hiddens[at].reshape(part * rows_dev, hiddens.shape[2])
            total[...] += dot(lhs, rhs, TN)
            return carry

        lax.fori_loop(0, 4, one, 0)

    wide.start()
    thin.start()
    pass_z(0)
    for copy in kept:
        copy.start()
    number_rows()
    make_shifts()
    for direction in (0, 1):
        wide.take_y(0, direction, direction)
    wide.take_x(0)
    for direction in (0, 1):
        wide.take_y(0, 1 - direction, direction)
    wide.take_x(1)
    pass_z(1)
    for half in (0, 1):
        for direction in (half, 1 - half):
            thin.take_y(0, half, direction)
    for direction in (0, 1):
        wide.take_far(0, direction)
        thin.take_far(0, direction)
    for direction in (0, 1):
        wide.take_y(1, direction, direction)
    for direction in (0, 1):
        wide.take_y(1, 1 - direction, direction)
    pass_z(2)
    for step in (0, 1, -1, 2):
        for half in (0, 1):
            thin.take_x(step, half)
    for direction in (0, 1):
        wide.take_far(1, direction)
    thin.take_shared()
    wide.take_shared()
    kept[0].wait()
    kept[1].wait()
    loads[0].wait()
    own_rows()
    own_packed = pltpu.make_async_copy(
        packed.at[place.z], blocks.at[:, place.z, place.t], own_sems.at[5]
    )
    own_packed.start()
    to_all_z(lambda step: packed.at[z_at(step)], blocks.at[:, place.z, place.t], packed_base)
    pass_z(3)
    inv_rms = pick_rows()
    make_terms(inv_rms)
    from_all_z(lambda step: blocks.at[:, z_at(step), place.t], packed_base)
    own_packed.wait()
    theirs.start((0,))
    ours.start((1,))
    to_all_z(lambda step: terms.at[z_at(step)], terms_in.at[place.z], terms_base)
    products = make_back(0, tiles, jnp.zeros((rows_dev, 1), f32))
    ours.take_y(0, 1, 1)
    theirs.take_y(0, 0, 0)
    ours.take_y(0, 1, 0)
    theirs.take_y(0, 0, 1)
    theirs.take_x(0)
    ours.take_far(0, 1)
    ours.take_x(0, 1)
    theirs.take_far(0, 0)
    theirs.take_y(1, 0, 0)
    theirs.take_y(1, 0, 1)
    for step in (1, -1):
        ours.take_x(step, 1)
    theirs.take_far(1, 0)
    ours.take_x(2, 1)
    for direction, step in ((0, -1), (1, 1)):
        sends.arrived(z_slot(4 * step, direction), z_base + direction * 4 + 3, place.at_z(step))
    kept[2].wait()
    theirs.take_shared((0,))
    connector_part(1 - place.xl)
    away[...] = total[...].astype(bf16)
    sends.send(
        away.at[pl.ds(0, piece_rows)], away_in.at[pl.ds(0, piece_rows)], x_base, over_x
    )
    from_all_z(lambda step: terms_in.at[z_at(step)], terms_base)
    terms_in[place.z] = terms[place.z]

    def add_up(i, carry):
        tile = tile_of(i)
        added = jnp.sum(terms_in[:, :, tile].astype(f32), axis=0)
        sums[:, tile] = added
        sums_out[:, tile] = added.astype(bf16)
        return carry

    lax.fori_loop(0, tiles, add_up, 0)
    sends.send(sums_out, sums_in, x_base + 1, over_x)
    loads[1].wait()
    make_hidden_grad(inv_rms, products)
    ours.take_shared((1,))
    connector_part(place.xl)
    own_sum_ref[...] = total[0:piece_rows, :]
    sends.arrived(sums_in, x_base + 1, over_x)
    weight_sums_ref[...] = sums[...] + sums_in[...].astype(f32)
    sends.arrived(away_in.at[pl.ds(0, piece_rows)], x_base, over_x)
    swapped_ref[...] = away_in[0:piece_rows, :]
    sends.drain()


def close(factor, hidden_ref, own_ref, swapped_ref, sums_ref, hidden_grad_ref, connector_grad_ref, weight_grad_ref):
    hidden_grad_ref[...] = hidden_ref[...]
    connector_grad_ref[...] = (own_ref[...] + swapped_ref[...].astype(jnp.float32)) * factor
    sums = sums_ref[...]
    mine = jnp.where(lax.axis_index("dp") < NZ, sums[0:4], sums[4:8])
    weight_grad_ref[...] = mine * factor


VMEM = pl.BlockSpec(memory_space=pltpu.VMEM)
ANY = pl.BlockSpec(memory_space=pl.ANY)


def on_device(hidden, connector, routing, talker_in, norm_gain, kv_weight, kv_grad):
    n_dp = lax.axis_size("dp")
    n_tensor = lax.axis_size("tensor")
    rows_dev, d_dev = hidden.shape
    capacity, width = talker_in.shape
    kv_width = kv_grad.shape[1]
    slots = n_tensor * capacity
    share = rows_dev // n_tensor
    per_dev = kv_width // (n_dp * n_tensor)
    bf16, f32 = jnp.bfloat16, jnp.float32

    keys = 4 * GROUP_KEYS + 3 * NZ + 2
    hidden_rows, own_sum, swapped, weight_sums = pl.pallas_call(
        whole,
        out_shape=(
            jax.ShapeDtypeStruct((rows_dev, d_dev), bf16),
            jax.ShapeDtypeStruct((width // n_dp, d_dev), f32),
            jax.ShapeDtypeStruct((width // n_dp, d_dev), bf16),
            jax.ShapeDtypeStruct((8, width), f32),
        ),
        in_specs=[VMEM] * 5 + [ANY] * 2,
        out_specs=[VMEM] * 4,
        scratch_shapes=[
            pltpu.VMEM((n_tensor, capacity, width), bf16),
            pltpu.VMEM((n_tensor, capacity, kv_width), bf16),
            pltpu.VMEM((NZ, rows_dev, d_dev), bf16),
            pltpu.VMEM(kv_weight.shape, bf16),
            pltpu.VMEM(connector.shape, bf16),
            pltpu.VMEM((share, width), f32),
            pltpu.VMEM((share, width), f32),
            pltpu.VMEM((share, width), bf16),
            pltpu.VMEM((NZ, 2, share, BLOCK), bf16),
            pltpu.VMEM((2, NZ, n_tensor, share, BLOCK), bf16),
            pltpu.VMEM((8, WINDOW, BLOCK), bf16),
            pltpu.VMEM((rows_dev, slots), bf16),
            pltpu.VMEM((rows_dev, width), bf16),
            pltpu.VMEM((rows_dev, kv_width), bf16),
            pltpu.VMEM((rows_dev, width), f32),
            pltpu.VMEM((n_dp * per_dev, rows_dev), bf16),
            pltpu.VMEM((NZ, 8, width), bf16),
            pltpu.VMEM((NZ, 8, width), bf16),
            pltpu.VMEM((BLOCK, d_dev), bf16),
            pltpu.VMEM((BLOCK, d_dev), bf16),
            pltpu.VMEM((8, width), f32),
            pltpu.VMEM((8, width), bf16),
            pltpu.VMEM((8, width), bf16),
            pltpu.VMEM((BLOCK, d_dev), f32),
            pltpu.VMEM((1, width), f32),
            pltpu.SemaphoreType.DMA((keys,)),
            pltpu.SemaphoreType.DMA((keys,)),
            pltpu.SemaphoreType.DMA((6,)),
        ],
        compiler_params=pltpu.CompilerParams(
            collective_id=0, has_side_effects=True, vmem_limit_bytes=60 * 1024 * 1024
        ),
    )(
        talker_in,
        kv_grad,
        hidden,
        norm_gain.reshape(width // 128, 128),
        routing.T,
        kv_weight,
        connector,
    )
    factor = 1.0 / math.sqrt(rows_dev * n_dp)
    hidden_grad, connector_grad, weight_grad = pl.pallas_call(
        functools.partial(close, factor),
        out_shape=(
            jax.ShapeDtypeStruct((rows_dev, d_dev), bf16),
            jax.ShapeDtypeStruct((width // n_dp, d_dev), f32),
            jax.ShapeDtypeStruct((per_dev, width), f32),
        ),
        in_specs=[VMEM] * 4,
        out_specs=[VMEM] * 3,
    )(hidden_rows, own_sum, swapped, weight_sums)
    return (hidden_grad, connector_grad.T, weight_grad.T)


def solution(mesh):
    return jax.shard_map(
        on_device,
        mesh=mesh,
        in_specs=(
            P("dp", "tensor"),
            P("tensor", None),
            P("dp", None),
            P(("dp", "tensor"), None),
            P(),
            P(),
            P(("dp", "tensor"), None),
        ),
        out_specs=(P("dp", "tensor"), P("tensor", "dp"), P(None, ("dp", "tensor"))),
        check_vma=False,
    )
```
